256 devices in a mesh: chan: 64 (over z, x_hi, y), sky: 4 (over x_lo, core).
Axes of the slice: x: 4 (x_hi: 2, x_lo: 2; x = x_hi * 2 + x_lo), y: 4, z: 8, core: 2. Of those that a mesh axis runs over, the one named last changes fastest.
Arguments:
- cube: float32 [512, 1024, 512], P('sky', 'chan'), may hold values from -6 to 6
- shifts: int32 [256], P('chan'), may hold values from -12 to 12
- halfwidth: int32 [256], P('chan'), may hold values from 1 to 4
- taps: float32 [1024, 9], P('chan'), may hold values from 0.1 to 1
- beam_rows: float32 [512, 512], replicated, as said below
- beam_cols: float32 [512, 512], replicated, as said below
Outputs:
- regridded: float32 [512, 1024, 512], P('sky', 'chan')
The draws below stay inside these ranges and needn't reach their ends.
Inputs may be any that keep to these rules, and one draw needn't show every extreme that they name: beam_rows[i, j] is zero where |i - j| > 8; its diagonal exceeds the sum of the other entries of its row. beam_cols[i, j] is zero where |i - j| > 8; its diagonal exceeds the sum of the other entries of its row.
All inputs are finite; a program needn't handle non-finite values.
Results may differ from the reference program's by a relative error of at most 0.0003.
Values sent between devices are 32-bit elements; how exact they have to be, the bound alone decides.
A program may use at most 64 MiB of HBM per device.

```python
import math
import jax
import jax.numpy as jnp
from jax import lax

H = 512
W = 512
CH_DEV = 16
BLK = 4
S_MAX = 12
RADIUS = 4
BAND = 8
NCH = 1024
NBLK = 256


def banded_matrix(key, count):
    rows = jnp.arange(count)[:, None]
    cols = jnp.arange(count)[None, :]
    inside = (jnp.abs(rows - cols) <= BAND) & (rows != cols)
    values = jax.random.uniform(key, (count, count), jnp.float32, 0.0, 0.06)
    return jnp.where(inside, values, 0.0) + jnp.eye(count, dtype=jnp.float32)


def draw_beam_rows(key, part):
    return banded_matrix(jax.random.fold_in(key, 11), H)


def draw_beam_cols(key, part):
    return banded_matrix(jax.random.fold_in(key, 23), W)


def place_ends(drawn, stream_key, smallest, high):
    place = [jax.random.randint(jax.random.fold_in(stream_key, axis), (), 0, length) for axis, length in enumerate(drawn.shape)]
    main_axis = drawn.shape.index(max(drawn.shape))
    next_to = place[:main_axis] + [(place[main_axis] + 1) % drawn.shape[main_axis]] + place[main_axis + 1:]
    return drawn.at[tuple(place)].set(smallest).at[tuple(next_to)].set(high)


def steps_of(key, dims, shards, least, top_value):
    def one(axis_at, parts):
        steps = jax.random.uniform(jax.random.fold_in(jax.random.fold_in(key, 6), axis_at), (parts,), jnp.float32, least / len(shards), top_value / len(shards))
        return jnp.repeat(jnp.exp(steps), dims[axis_at] // parts).reshape((-1,) + (1,) * (len(dims) - axis_at - 1))

    loudness = one(*shards[0])
    for cut in shards[1:]:
        loudness = loudness * one(*cut)
    return loudness


def bell_draw(key, dims, width, bound, cuts=(), kind=jnp.bfloat16):
    loudness = steps_of(key, dims, cuts, -0.22, 0.18) if cuts else 1.0
    entries = jax.random.normal(key, dims, jnp.float32) * width * loudness
    return jnp.minimum(jnp.maximum(entries, -bound), bound).astype(kind)


def setup_inputs(seed: int = 0) -> dict:
    keys = jax.random.split(jax.random.key(seed), 7)
    cube = bell_draw(keys[0], (H, NCH, W), 1.0, 6.0, ((0, 4), (1, 64)), jnp.float32)
    shifts = place_ends(jax.random.randint(keys[1], (NBLK,), 0 - S_MAX, S_MAX + 1), jax.random.fold_in(keys[1], 1), 0 - S_MAX, S_MAX).astype(jnp.int32)
    halfwidth = place_ends(jax.random.randint(keys[2], (NBLK,), 1, RADIUS + 1), jax.random.fold_in(keys[2], 1), 1, RADIUS).astype(jnp.int32)
    taps = jnp.clip(jnp.exp(math.log(1.0) - 2.3025851 * jax.random.uniform(keys[3], (NCH, 2 * RADIUS + 1), jnp.float32) ** steps_of(keys[3], (NCH, 2 * RADIUS + 1), ((0, 64),), -0.2, 0.2)), 0.1, 1.0)
    beam_rows = draw_beam_rows(jax.random.fold_in(keys[6], 71), 0)
    beam_cols = draw_beam_cols(jax.random.fold_in(keys[6], 71), 0)
    return {"cube": cube, "shifts": shifts, "halfwidth": halfwidth, "taps": taps, "beam_rows": beam_rows, "beam_cols": beam_cols}


def reference(cube, shifts, halfwidth, taps, beam_rows, beam_cols):
    reach = S_MAX + RADIUS
    taps_count = 2 * RADIUS + 1
    chan_ids = jnp.arange(NCH, dtype=jnp.int32)
    block_ids = chan_ids // BLK
    offsets = jnp.take(shifts, block_ids)
    limits = jnp.take(halfwidth, block_ids)
    tap_ids = jnp.arange(taps_count, dtype=jnp.int32)
    active = jnp.abs(tap_ids - RADIUS)[None, :] <= limits[:, None]
    masked = jnp.where(active, taps, jnp.float32(0.0))
    weights = masked / jnp.sum(masked, axis=1, keepdims=True)
    local_ids = jnp.arange(CH_DEV, dtype=jnp.int32)
    source = local_ids[:, None] + reach + offsets.reshape(NCH // CH_DEV, CH_DEV)[:, :, None] + tap_ids[None, None, :] - RADIUS
    padded = jnp.pad(cube, ((0, 0), (reach, reach), (0, 0)))
    groups = NCH // CH_DEV

    def one_group(inputs):
        group, group_weights, group_source = inputs
        slab = lax.dynamic_slice_in_dim(padded, (group * CH_DEV).astype(jnp.int32), CH_DEV + 2 * reach, 1)
        interp = jnp.zeros((H, CH_DEV, W), jnp.float32)
        for tap in range(taps_count):
            picked = jnp.take(slab, group_source[:, tap], axis=1)
            interp = interp + group_weights[:, tap][None, :, None] * picked
        smoothed = jnp.einsum("hcw,vw->hcv", interp, beam_cols, precision=lax.Precision.HIGHEST)
        return jnp.einsum("gh,hcv->gcv", beam_rows, smoothed, precision=lax.Precision.HIGHEST)

    stacked = lax.map(one_group, (jnp.arange(groups, dtype=jnp.int32), weights.reshape(groups, CH_DEV, taps_count), source))
    return jnp.transpose(stacked, (1, 0, 2, 3)).reshape(H, NCH, W)
```

```python
import functools

import jax
import jax.numpy as jnp
from jax import lax
from jax.experimental import pallas as pl
from jax.experimental.pallas import tpu as pltpu
from jax.sharding import PartitionSpec as P

BLK = 4
S_MAX = 12
RADIUS = 4
BAND = 8
MESH = pl.DeviceIdType.MESH
BF16 = jnp.bfloat16
F32 = jnp.float32


def split(x):
    high = x.astype(BF16)
    return high, (x - high.astype(F32)).astype(BF16)


def dot(a, b):
    return jnp.dot(a, b, preferred_element_type=F32)


def iota(shape, dim):
    return lax.broadcasted_iota(jnp.int32, shape, dim)


def kernel(
    groups, skies, cube, shifts, halfwidth, taps, beam_rows, beam_cols, out,
    own, left_in, right_in, spread, spread_low, edge_out, edge_in, cols, cols_pair, rows, row_ops, chan_op,
    local_sem, send_sem, recv_sem, edge_send, edge_recv,
):
    chunks, size, width = cube.shape
    chans = size // BAND
    reach = S_MAX + RADIUS
    group, sky = lax.axis_index("chan"), lax.axis_index("sky")
    right, left = lax.rem(group + 1, groups), lax.rem(group + groups - 1, groups)
    has_up, has_down = sky > 0, sky < skies - 1

    barrier = pltpu.get_barrier_semaphore()
    pl.semaphore_signal(barrier, inc=1, device_id={"chan": left}, device_id_type=MESH)
    pl.semaphore_signal(barrier, inc=1, device_id={"chan": right}, device_id_type=MESH)

    @pl.when(has_up)
    def _():
        pl.semaphore_signal(barrier, inc=1, device_id={"sky": sky - 1}, device_id_type=MESH)

    @pl.when(has_down)
    def _():
        pl.semaphore_signal(barrier, inc=1, device_id={"sky": sky + 1}, device_id_type=MESH)

    pl.semaphore_wait(barrier, 2 + has_up.astype(jnp.int32) + has_down.astype(jnp.int32))

    def to_right(at):
        return pltpu.make_async_remote_copy(
            src_ref=cube.at[at], dst_ref=left_in.at[at], send_sem=send_sem.at[0, at], recv_sem=recv_sem.at[0, at],
            device_id={"chan": right}, device_id_type=MESH)

    def to_left(at):
        return pltpu.make_async_remote_copy(
            src_ref=cube.at[at], dst_ref=right_in.at[at], send_sem=send_sem.at[1, at], recv_sem=recv_sem.at[1, at],
            device_id={"chan": left}, device_id_type=MESH)

    @pl.loop(0, chunks // 2)
    def _(step):
        for at in (step, chunks - 1 - step):
            to_right(at).start()
            to_left(at).start()

    height = chunks * BAND
    local = [
        pltpu.make_async_copy(cube, own, local_sem.at[0]),
        pltpu.make_async_copy(beam_cols, cols, local_sem.at[1]),
    ]
    for part in range(3):
        block = lax.rem(sky + skies + part - 1, skies)
        local.append(pltpu.make_async_copy(
            beam_rows.at[pl.ds(pl.multiple_of(sky * height, height), height),
                         pl.ds(pl.multiple_of(block * height, height), height)],
            rows.at[:, pl.ds(part * height, height)], local_sem.at[2 + part]))
    for copy in local:
        copy.start()

    chan = iota((chans, 128), 0)
    place = iota((chans, 128), 1)
    offsets = jnp.zeros((chans, 128), jnp.int32)
    limits = jnp.zeros((chans, 2 * RADIUS + 1), jnp.int32)
    for block in range(chans // BLK):
        offsets = jnp.where(chan // BLK == block, shifts[block], offsets)
        limits = jnp.where(iota(limits.shape, 0) // BLK == block, halfwidth[block], limits)
    masked = jnp.where(jnp.abs(iota(limits.shape, 1) - RADIUS) <= limits, taps[...], 0.0)
    weights = masked / jnp.sum(masked, axis=1, keepdims=True)
    band = jnp.zeros((chans, 128), F32)
    for tap in range(2 * RADIUS + 1):
        band = band + jnp.where(place == chan + reach + offsets + (tap - RADIUS), weights[:, tap:tap + 1], 0.0)
    first = jnp.where(group == 0, chans, 0)
    last = jnp.where(group == groups - 1, 2 * chans, 3 * chans)
    band = jnp.where((place >= first) & (place < last), band, 0.0)
    column = iota((128, 3 * size), 1)
    pick = (iota((128, 3 * size), 0) == column // size * chans + column % chans).astype(BF16)
    same_row = iota((size, 3 * size), 0) // chans == iota((size, 3 * size), 1) % size // chans
    for at, part in enumerate(split(band)):
        wide = jnp.concatenate([dot(part, pick)] * BAND, axis=0)
        chan_op[pl.ds(at * size, size), :] = jnp.where(same_row, wide, 0.0).astype(BF16)

    for copy in local:
        copy.wait()
    high, low = split(cols[...])
    cols_pair[0] = high
    cols_pair[1] = low

    pick = (iota((128, 3 * size), 0) == column // chans).astype(BF16)
    same_chan = iota((size, 3 * size), 0) % chans == iota((size, 3 * size), 1) % chans
    for at in range(chunks):
        start = height + (at - 1) * BAND
        near = rows[pl.ds(at * BAND, BAND), start:start + 3 * BAND]
        near = jnp.concatenate([near, jnp.zeros((BAND, 128 - 3 * BAND), F32)], axis=1)
        high, low = split(near)
        for half, part in enumerate((high, low)):
            wide = dot(part, pick)
            wide = jnp.broadcast_to(wide[:, None, :], (BAND, chans, 3 * size)).reshape(size, 3 * size)
            row_ops[at, pl.ds(half * size, size), :] = jnp.where(same_chan, wide, 0.0).astype(BF16)

    def keep(at, value):
        high, low = split(value)
        spread[at] = high
        spread_low[at] = low

    def smooth(at):
        to_right(at).wait_recv()
        to_left(at).wait_recv()
        total = jnp.zeros((size, width), F32)
        for part, ref in enumerate((left_in, own, right_in)):
            high, low = split(ref[at])
            op = chan_op[:, part * size:(part + 1) * size]
            both = dot(op, high)
            total = total + (both[:size] + both[size:] + dot(op[:size], low))
        high, low = split(total)
        across = (((1,), (1,)), ((), ()))
        both = lax.dot_general(jnp.concatenate([high, low], axis=0), cols_pair[0], across, preferred_element_type=F32)
        return both[:size] + both[size:] + lax.dot_general(high, cols_pair[1], across, preferred_element_type=F32)

    def finish(at):
        op = row_ops[at]
        both = dot(op, spread[pl.ds(at, 3)].reshape(3 * size, width))
        out[at] = both[:size] + both[size:] + dot(op[:size], spread_low[pl.ds(at, 3)].reshape(3 * size, width))

    for side, at in enumerate((0, chunks - 1)):
        value = smooth(at)
        edge_out[side] = value
        keep(at + 1, value)

    @pl.loop(1, 2)
    def _(step):
        for at in (step, chunks - 1 - step):
            keep(at + 1, smooth(at))

    up = pltpu.make_async_remote_copy(
        src_ref=edge_out.at[0], dst_ref=edge_in.at[1], send_sem=edge_send.at[0], recv_sem=edge_recv.at[1],
        device_id={"sky": sky - 1}, device_id_type=MESH)
    down = pltpu.make_async_remote_copy(
        src_ref=edge_out.at[1], dst_ref=edge_in.at[0], send_sem=edge_send.at[1], recv_sem=edge_recv.at[0],
        device_id={"sky": sky + 1}, device_id_type=MESH)

    @pl.when(has_up)
    def _():
        up.start()

    @pl.when(has_down)
    def _():
        down.start()

    @pl.loop(2, chunks // 2)
    def _(step):
        for at in (step, chunks - 1 - step):
            keep(at + 1, smooth(at))
        finish(step - 1)
        finish(chunks - step)

    for at in (chunks // 2 - 1, chunks // 2):
        finish(at)

    @pl.when(has_up)
    def _():
        down.wait_recv()
        keep(0, edge_in[0])
        up.wait_send()

    @pl.when(has_down)
    def _():
        up.wait_recv()
        keep(chunks + 1, edge_in[1])
        down.wait_send()

    @pl.when(jnp.logical_not(has_up))
    def _():
        keep(0, jnp.zeros((size, width), F32))

    @pl.when(jnp.logical_not(has_down))
    def _():
        keep(chunks + 1, jnp.zeros((size, width), F32))

    finish(0)
    finish(chunks - 1)

    @pl.loop(0, chunks)
    def _(at):
        to_right(at).wait_send()
        to_left(at).wait_send()


def solution(mesh):
    groups, skies = mesh.shape["chan"], mesh.shape["sky"]

    def per_device(cube, shifts, halfwidth, taps, beam_rows, beam_cols):
        height, chans, width = cube.shape
        chunks, size = height // BAND, BAND * chans
        anywhere = pl.BlockSpec(memory_space=pl.ANY)
        vmem = pl.BlockSpec(memory_space=pltpu.VMEM)
        smem = pl.BlockSpec(memory_space=pltpu.SMEM)
        whole = (chunks, size, width)
        result = pl.pallas_call(
            functools.partial(kernel, groups, skies),
            out_shape=jax.ShapeDtypeStruct(whole, F32),
            in_specs=[anywhere, smem, smem, vmem, anywhere, anywhere],
            out_specs=vmem,
            scratch_shapes=[
                pltpu.VMEM(whole, F32),
                pltpu.VMEM(whole, F32),
                pltpu.VMEM(whole, F32),
                pltpu.VMEM((chunks + 2, size, width), BF16),
                pltpu.VMEM((chunks + 2, size, width), BF16),
                pltpu.VMEM((2, size, width), F32),
                pltpu.VMEM((2, size, width), F32),
                pltpu.VMEM((width, width), F32),
                pltpu.VMEM((2, width, width), BF16),
                pltpu.VMEM((height, 3 * height), F32),
                pltpu.VMEM((chunks, 2 * size, 3 * size), BF16),
                pltpu.VMEM((2 * size, 3 * size), BF16),
                pltpu.SemaphoreType.DMA((5,)),
                pltpu.SemaphoreType.DMA((2, chunks)),
                pltpu.SemaphoreType.DMA((2, chunks)),
                pltpu.SemaphoreType.DMA((2,)),
                pltpu.SemaphoreType.DMA((2,)),
            ],
            compiler_params=pltpu.CompilerParams(collective_id=0, has_side_effects=True, vmem_limit_bytes=48 << 20),
            name="regrid",
        )(cube.reshape(whole), shifts, halfwidth, taps, beam_rows, beam_cols)
        return result.reshape(cube.shape)

    return jax.shard_map(
        per_device,
        mesh=mesh,
        in_specs=(P("sky", "chan", None), P("chan"), P("chan"), P("chan", None), P(), P()),
        out_specs=P("sky", "chan", None),
        check_vma=False,
    )
```

```python
import functools

import jax
import jax.numpy as jnp
from jax import lax
from jax.experimental import pallas as pl
from jax.experimental.pallas import tpu as pltpu
from jax.sharding import PartitionSpec as P

BLK = 4
S_MAX = 12
RADIUS = 4
BAND = 8
MESH = pl.DeviceIdType.MESH
BF16 = jnp.bfloat16
F32 = jnp.float32


def split(x):
    high = x.astype(BF16)
    return high, (x - high.astype(F32)).astype(BF16)


def dot(a, b):
    return jnp.dot(a, b, preferred_element_type=F32)


def iota(shape, dim):
    return lax.broadcasted_iota(jnp.int32, shape, dim)


def kernel(
    groups, skies, cube, shifts_in, halfwidth_in, taps_in, beam_rows, beam_cols, out,
    shifts, halfwidth, taps, own, left_in, right_in, spread, spread_low, tail_op, edge_out, edge_in, cols, cols_pair, rows, row_ops, chan_op,
    local_sem, send_sem, recv_sem, edge_send, edge_recv,
):
    chunks, size, width = cube.shape
    chans = size // BAND
    reach = S_MAX + RADIUS
    group, sky = lax.axis_index("chan"), lax.axis_index("sky")
    has_left, has_right = group > 0, group < groups - 1
    has_up, has_down = sky > 0, sky < skies - 1
    sides = ((has_left, {"chan": group - 1}), (has_right, {"chan": group + 1}),
             (has_up, {"sky": sky - 1}), (has_down, {"sky": sky + 1}))

    barrier = pltpu.get_barrier_semaphore()
    waits = 0
    for there, device in sides:
        @pl.when(there)
        def _():
            pl.semaphore_signal(barrier, inc=1, device_id=device, device_id_type=MESH)

        waits = waits + there.astype(jnp.int32)
    pl.semaphore_wait(barrier, waits)

    def to_right(at):
        return pltpu.make_async_remote_copy(
            src_ref=cube.at[at], dst_ref=left_in.at[at], send_sem=send_sem.at[0, at], recv_sem=recv_sem.at[0, at],
            device_id={"chan": group + 1}, device_id_type=MESH)

    def to_left(at):
        return pltpu.make_async_remote_copy(
            src_ref=cube.at[at], dst_ref=right_in.at[at], send_sem=send_sem.at[1, at], recv_sem=recv_sem.at[1, at],
            device_id={"chan": group - 1}, device_id_type=MESH)

    @pl.loop(0, chunks // 2)
    def _(step):
        for at in (step, chunks - 1 - step):
            @pl.when(has_right)
            def _():
                to_right(at).start()

            @pl.when(has_left)
            def _():
                to_left(at).start()

    height = chunks * BAND
    local = [
        pltpu.make_async_copy(cube, own, local_sem.at[0]),
        pltpu.make_async_copy(beam_cols, cols, local_sem.at[1]),
        pltpu.make_async_copy(shifts_in, shifts, local_sem.at[5]),
        pltpu.make_async_copy(halfwidth_in, halfwidth, local_sem.at[6]),
        pltpu.make_async_copy(taps_in, taps, local_sem.at[7]),
    ]
    for part in range(3):
        block = lax.rem(sky + skies + part - 1, skies)
        local.append(pltpu.make_async_copy(
            beam_rows.at[pl.ds(pl.multiple_of(sky * height, height), height),
                         pl.ds(pl.multiple_of(block * height, height), height)],
            rows.at[:, pl.ds(part * height, height)], local_sem.at[2 + part]))
    for copy in local:
        copy.start()

    @pl.when(jnp.logical_not(has_left))
    def _():
        left_in[...] = jnp.zeros(left_in.shape, F32)

    @pl.when(jnp.logical_not(has_right))
    def _():
        right_in[...] = jnp.zeros(right_in.shape, F32)

    for copy in local:
        copy.wait()

    chan = iota((chans, 128), 0)
    place = iota((chans, 128), 1)
    offsets = jnp.zeros((chans, 128), jnp.int32)
    limits = jnp.zeros((chans, 2 * RADIUS + 1), jnp.int32)
    for block in range(chans // BLK):
        offsets = jnp.where(chan // BLK == block, shifts[block], offsets)
        limits = jnp.where(iota(limits.shape, 0) // BLK == block, halfwidth[block], limits)
    masked = jnp.where(jnp.abs(iota(limits.shape, 1) - RADIUS) <= limits, taps[...], 0.0)
    weights = masked / jnp.sum(masked, axis=1, keepdims=True)
    band = jnp.zeros((chans, 128), F32)
    for tap in range(2 * RADIUS + 1):
        band = band + jnp.where(place == chan + reach + offsets + (tap - RADIUS), weights[:, tap:tap + 1], 0.0)
    column = iota((128, 3 * size), 1)
    pick = (iota((128, 3 * size), 0) == column // size * chans + column % chans).astype(BF16)
    same_row = iota((size, 3 * size), 0) // chans == iota((size, 3 * size), 1) % size // chans
    for at, part in enumerate(split(band)):
        wide = jnp.concatenate([dot(part, pick)] * BAND, axis=0)
        chan_op[pl.ds(at * size, size), :] = jnp.where(same_row, wide, 0.0).astype(BF16)

    high, low = split(cols[...])
    cols_pair[0] = high
    cols_pair[1] = low

    pick = (iota((128, 3 * size), 0) == column // chans).astype(BF16)
    same_chan = iota((size, 3 * size), 0) % chans == iota((size, 3 * size), 1) % chans
    for at in range(chunks):
        start = height + (at - 1) * BAND
        near = rows[pl.ds(at * BAND, BAND), start:start + 3 * BAND]
        near = jnp.concatenate([near, jnp.zeros((BAND, 128 - 3 * BAND), F32)], axis=1)
        high, low = split(near)
        for half, part in enumerate((high, low)):
            wide = dot(part, pick)
            wide = jnp.broadcast_to(wide[:, None, :], (BAND, chans, 3 * size)).reshape(size, 3 * size)
            row_ops[at, pl.ds(half * size, size), :] = jnp.where(same_chan, wide, 0.0).astype(BF16)

    def keep(at, value):
        high, low = split(value)
        spread[at] = high
        spread_low[at] = low

    def arrive(at):
        @pl.when(has_left)
        def _():
            to_right(at).wait_recv()

        @pl.when(has_right)
        def _():
            to_left(at).wait_recv()

    def blend(part, ref, at):
        high, low = split(ref[at])
        op = chan_op[:, part * size:(part + 1) * size]
        both = dot(op, high)
        return both[:size] + both[size:] + dot(op[:size], low)

    def across(total):
        high, low = split(total)
        dims = (((1,), (1,)), ((), ()))
        both = lax.dot_general(jnp.concatenate([high, low], axis=0), cols_pair[0], dims, preferred_element_type=F32)
        return both[:size] + both[size:] + lax.dot_general(high, cols_pair[1], dims, preferred_element_type=F32)

    def smooth(at):
        arrive(at)
        return across(blend(1, own, at) + blend(0, left_in, at) + blend(2, right_in, at))

    def finish(at):
        op = row_ops[at]
        both = dot(op, spread[pl.ds(at, 3)].reshape(3 * size, width))
        out[at] = both[:size] + both[size:] + dot(op[:size], spread_low[pl.ds(at, 3)].reshape(3 * size, width))

    for side, at in enumerate((0, chunks - 1)):
        value = smooth(at)
        edge_out[side] = value
        keep(at + 1, value)

    for at in (1, chunks - 2):
        keep(at + 1, smooth(at))

    up = pltpu.make_async_remote_copy(
        src_ref=edge_out.at[0], dst_ref=edge_in.at[1], send_sem=edge_send.at[0], recv_sem=edge_recv.at[1],
        device_id={"sky": sky - 1}, device_id_type=MESH)
    down = pltpu.make_async_remote_copy(
        src_ref=edge_out.at[1], dst_ref=edge_in.at[0], send_sem=edge_send.at[1], recv_sem=edge_recv.at[0],
        device_id={"sky": sky + 1}, device_id_type=MESH)

    @pl.when(has_up)
    def _():
        up.start()

    @pl.when(has_down)
    def _():
        down.start()

    last = chunks // 2
    keep(last + 1, jnp.zeros((size, width), F32))
    for place in range(3):
        for half in range(2):
            tail_op[pl.ds((3 * half + place) * size, size), :] = row_ops[
                last - 1 + place, pl.ds(half * size, size), (2 - place) * size:(3 - place) * size]

    @pl.loop(2, last - 1)
    def _(step):
        for at in (step, chunks - 1 - step):
            keep(at + 1, smooth(at))
        finish(step - 1)
        finish(chunks - step)

    @pl.when(has_up)
    def _():
        down.wait_recv()
        keep(0, edge_in[0])

    @pl.when(has_down)
    def _():
        up.wait_recv()
        keep(chunks + 1, edge_in[1])

    @pl.when(jnp.logical_not(has_up))
    def _():
        keep(0, jnp.zeros((size, width), F32))

    @pl.when(jnp.logical_not(has_down))
    def _():
        keep(chunks + 1, jnp.zeros((size, width), F32))

    finish(0)
    finish(chunks - 1)
    keep(last, smooth(last - 1))
    ready = blend(1, own, last)
    for at in (last - 2, last + 1, last - 1, last):
        finish(at)

    arrive(last)
    high, low = split(across(ready + blend(0, left_in, last) + blend(2, right_in, last)))
    three = 3 * size
    both = dot(tail_op[...], high)
    share = both[:three] + both[three:] + dot(tail_op[:three, :], low)
    for place in range(3):
        out[last - 1 + place] += share[place * size:(place + 1) * size]

    @pl.when(has_up)
    def _():
        up.wait_send()

    @pl.when(has_down)
    def _():
        down.wait_send()

    @pl.loop(0, chunks)
    def _(at):
        @pl.when(has_right)
        def _():
            to_right(at).wait_send()

        @pl.when(has_left)
        def _():
            to_left(at).wait_send()


def solution(mesh):
    groups, skies = mesh.shape["chan"], mesh.shape["sky"]

    def per_device(cube, shifts, halfwidth, taps, beam_rows, beam_cols):
        height, chans, width = cube.shape
        chunks, size = height // BAND, BAND * chans
        stay = pl.BlockSpec(memory_space=pltpu.HBM)
        whole = (chunks, size, width)
        result = pl.pallas_call(
            functools.partial(kernel, groups, skies),
            out_shape=pltpu.VMEM(whole, F32),
            in_specs=[stay] * 6,
            out_specs=pl.BlockSpec(memory_space=pltpu.VMEM),
            scratch_shapes=[
                pltpu.SMEM(shifts.shape, jnp.int32),
                pltpu.SMEM(halfwidth.shape, jnp.int32),
                pltpu.VMEM(taps.shape, F32),
                pltpu.VMEM(whole, F32),
                pltpu.VMEM(whole, F32),
                pltpu.VMEM(whole, F32),
                pltpu.VMEM((chunks + 2, size, width), BF16),
                pltpu.VMEM((chunks + 2, size, width), BF16),
                pltpu.VMEM((6 * size, size), BF16),
                pltpu.VMEM((2, size, width), F32),
                pltpu.VMEM((2, size, width), F32),
                pltpu.VMEM((width, width), F32),
                pltpu.VMEM((2, width, width), BF16),
                pltpu.VMEM((height, 3 * height), F32),
                pltpu.VMEM((chunks, 2 * size, 3 * size), BF16),
                pltpu.VMEM((2 * size, 3 * size), BF16),
                pltpu.SemaphoreType.DMA((8,)),
                pltpu.SemaphoreType.DMA((2, chunks)),
                pltpu.SemaphoreType.DMA((2, chunks)),
                pltpu.SemaphoreType.DMA((2,)),
                pltpu.SemaphoreType.DMA((2,)),
            ],
            compiler_params=pltpu.CompilerParams(collective_id=0, has_side_effects=True, vmem_limit_bytes=48 << 20),
            name="regrid",
        )(*(pltpu.with_memory_space_constraint(x, pltpu.HBM) for x in (
            cube.reshape(whole), shifts, halfwidth, taps, beam_rows, beam_cols)))
        return result.reshape(cube.shape)

    return jax.shard_map(
        per_device,
        mesh=mesh,
        in_specs=(P("sky", "chan", None), P("chan"), P("chan"), P("chan", None), P(), P()),
        out_specs=P("sky", "chan", None),
        check_vma=False,
    )
```

```python
import functools

import jax
import jax.numpy as jnp
from jax import lax
from jax.experimental import pallas as pl
from jax.experimental.pallas import tpu as pltpu
from jax.sharding import PartitionSpec as P

BLK = 4
S_MAX = 12
RADIUS = 4
BAND = 8
AHEAD = 2
RUN = 4
MESH = pl.DeviceIdType.MESH
BF16 = jnp.bfloat16
F32 = jnp.float32


def split(x):
    high = x.astype(BF16)
    return high, (x - high.astype(F32)).astype(BF16)


def dot(a, b):
    return jnp.dot(a, b, preferred_element_type=F32)


def iota(shape, dim):
    return lax.broadcasted_iota(jnp.int32, shape, dim)


def kernel(
    groups, skies, cube, shifts_in, halfwidth_in, taps_in, beam_rows, beam_cols, out,
    shifts, halfwidth, taps, own, left_in, right_in, spread, spread_low, tail_op, edge_out, edge_in, detour, cols, cols_pair, rows, row_ops, chan_op,
    local_sem, send_sem, recv_sem, edge_send, edge_recv,
):
    chunks, size, width = cube.shape
    chans = size // BAND
    reach = S_MAX + RADIUS
    group, sky = lax.axis_index("chan"), lax.axis_index("sky")
    has_left, has_right = group > 0, group < groups - 1
    has_up, has_down = sky > 0, sky < skies - 1
    spot = lax.rem(group, RUN)
    crosses = jnp.where(lax.rem(sky, 2) == 1, has_down, has_up)
    beyond = jnp.where(lax.rem(sky, 2) == 1, sky + 1, sky - 1)
    beside = jnp.where(spot == 0, group + 1, group - 1)
    detours = crosses & ((spot == 0) | (spot == RUN - 1)) & (beside < groups)
    served = jnp.where(spot == 1, group - 1, group + 1)
    relays = crosses & ((spot == 1) | (spot == RUN - 2)) & (served < groups)
    sides = ((has_left, {"chan": group - 1}), (has_right, {"chan": group + 1}),
             (has_up, {"sky": sky - 1}), (has_down, {"sky": sky + 1}))

    barrier = pltpu.get_barrier_semaphore()
    waits = 0
    for there, device in sides:
        @pl.when(there)
        def _():
            pl.semaphore_signal(barrier, inc=1, device_id=device, device_id_type=MESH)

        waits = waits + there.astype(jnp.int32)
    @pl.when(detours)
    def _():
        pl.semaphore_signal(barrier, inc=1, device_id={"chan": beside, "sky": beyond}, device_id_type=MESH)

    pl.semaphore_wait(barrier, waits + relays.astype(jnp.int32))

    def to_right(at):
        return pltpu.make_async_remote_copy(
            src_ref=cube.at[at], dst_ref=left_in.at[at], send_sem=send_sem.at[0, at], recv_sem=recv_sem.at[0, at],
            device_id={"chan": group + 1}, device_id_type=MESH)

    def to_left(at):
        return pltpu.make_async_remote_copy(
            src_ref=cube.at[at], dst_ref=right_in.at[at], send_sem=send_sem.at[1, at], recv_sem=recv_sem.at[1, at],
            device_id={"chan": group - 1}, device_id_type=MESH)

    def send(step):
        for at in (step, chunks - 1 - step):
            @pl.when(has_right)
            def _():
                to_right(at).start()

            @pl.when(has_left)
            def _():
                to_left(at).start()

    for step in range(AHEAD):
        send(step)

    height = chunks * BAND
    local = [
        pltpu.make_async_copy(cube, own, local_sem.at[0]),
        pltpu.make_async_copy(beam_cols, cols, local_sem.at[1]),
        pltpu.make_async_copy(shifts_in, shifts, local_sem.at[5]),
        pltpu.make_async_copy(halfwidth_in, halfwidth, local_sem.at[6]),
        pltpu.make_async_copy(taps_in, taps, local_sem.at[7]),
    ]
    for part in range(3):
        block = lax.rem(sky + skies + part - 1, skies)
        local.append(pltpu.make_async_copy(
            beam_rows.at[pl.ds(pl.multiple_of(sky * height, height), height),
                         pl.ds(pl.multiple_of(block * height, height), height)],
            rows.at[:, pl.ds(part * height, height)], local_sem.at[2 + part]))
    for copy in local:
        copy.start()

    @pl.when(jnp.logical_not(has_left))
    def _():
        left_in[...] = jnp.zeros(left_in.shape, F32)

    @pl.when(jnp.logical_not(has_right))
    def _():
        right_in[...] = jnp.zeros(right_in.shape, F32)

    for copy in local:
        copy.wait()

    chan = iota((chans, 128), 0)
    place = iota((chans, 128), 1)
    offsets = jnp.zeros((chans, 128), jnp.int32)
    limits = jnp.zeros((chans, 2 * RADIUS + 1), jnp.int32)
    for block in range(chans // BLK):
        offsets = jnp.where(chan // BLK == block, shifts[block], offsets)
        limits = jnp.where(iota(limits.shape, 0) // BLK == block, halfwidth[block], limits)
    masked = jnp.where(jnp.abs(iota(limits.shape, 1) - RADIUS) <= limits, taps[...], 0.0)
    weights = masked / jnp.sum(masked, axis=1, keepdims=True)
    band = jnp.zeros((chans, 128), F32)
    for tap in range(2 * RADIUS + 1):
        band = band + jnp.where(place == chan + reach + offsets + (tap - RADIUS), weights[:, tap:tap + 1], 0.0)
    column = iota((128, 3 * size), 1)
    pick = (iota((128, 3 * size), 0) == column // size * chans + column % chans).astype(BF16)
    same_row = iota((size, 3 * size), 0) // chans == iota((size, 3 * size), 1) % size // chans
    for at, part in enumerate(split(band)):
        wide = jnp.concatenate([dot(part, pick)] * BAND, axis=0)
        chan_op[pl.ds(at * size, size), :] = jnp.where(same_row, wide, 0.0).astype(BF16)

    high, low = split(cols[...])
    cols_pair[0] = high
    cols_pair[1] = low

    pick = (iota((128, 3 * size), 0) == column // chans).astype(BF16)
    same_chan = iota((size, 3 * size), 0) % chans == iota((size, 3 * size), 1) % chans
    for at in range(chunks):
        start = height + (at - 1) * BAND
        near = rows[pl.ds(at * BAND, BAND), start:start + 3 * BAND]
        near = jnp.concatenate([near, jnp.zeros((BAND, 128 - 3 * BAND), F32)], axis=1)
        high, low = split(near)
        for half, part in enumerate((high, low)):
            wide = dot(part, pick)
            wide = jnp.broadcast_to(wide[:, None, :], (BAND, chans, 3 * size)).reshape(size, 3 * size)
            row_ops[at, pl.ds(half * size, size), :] = jnp.where(same_chan, wide, 0.0).astype(BF16)

    def keep(at, value):
        high, low = split(value)
        spread[at] = high
        spread_low[at] = low

    def arrive(at):
        @pl.when(has_left)
        def _():
            to_right(at).wait_recv()

        @pl.when(has_right)
        def _():
            to_left(at).wait_recv()

    def blend(part, ref, at):
        high, low = split(ref[at])
        op = chan_op[:, part * size:(part + 1) * size]
        both = dot(op, high)
        return both[:size] + both[size:] + dot(op[:size], low)

    def across(total):
        high, low = split(total)
        dims = (((1,), (1,)), ((), ()))
        both = lax.dot_general(jnp.concatenate([high, low], axis=0), cols_pair[0], dims, preferred_element_type=F32)
        return both[:size] + both[size:] + lax.dot_general(high, cols_pair[1], dims, preferred_element_type=F32)

    def smooth(at):
        arrive(at)
        return across(blend(1, own, at) + blend(0, left_in, at) + blend(2, right_in, at))

    def finish(at):
        op = row_ops[at]
        both = dot(op, spread[pl.ds(at, 3)].reshape(3 * size, width))
        out[at] = both[:size] + both[size:] + dot(op[:size], spread_low[pl.ds(at, 3)].reshape(3 * size, width))

    for side, at in enumerate((0, chunks - 1)):
        value = smooth(at)
        edge_out[side] = value
        keep(at + 1, value)

    def edge(side, device):
        return pltpu.make_async_remote_copy(
            src_ref=edge_out.at[side], dst_ref=edge_in.at[1 - side], send_sem=edge_send.at[side],
            recv_sem=edge_recv.at[1 - side], device_id=device, device_id_type=MESH)

    up, down = edge(0, {"sky": sky - 1}), edge(1, {"sky": sky + 1})
    odd = lax.rem(sky, 2) == 1

    def first_leg(side):
        return pltpu.make_async_remote_copy(
            src_ref=edge_out.at[side], dst_ref=detour, send_sem=edge_send.at[side], recv_sem=edge_recv.at[2],
            device_id={"chan": beside}, device_id_type=MESH)

    def second_leg(side):
        return pltpu.make_async_remote_copy(
            src_ref=detour, dst_ref=edge_in.at[1 - side], send_sem=edge_send.at[2],
            recv_sem=edge_recv.at[1 - side], device_id={"chan": served, "sky": beyond}, device_id_type=MESH)

    for side, there, copy, turn in ((0, has_up, up, jnp.logical_not(odd)), (1, has_down, down, odd)):
        @pl.when(there & jnp.logical_not(detours & turn))
        def _():
            copy.start()

        @pl.when(detours & turn)
        def _():
            first_leg(side).start()

    for step in range(AHEAD, AHEAD + 2):
        send(step)
    for at in (1, chunks - 2):
        keep(at + 1, smooth(at))

    last = chunks // 2
    keep(last + 1, jnp.zeros((size, width), F32))
    for place in range(3):
        for half in range(2):
            tail_op[pl.ds((3 * half + place) * size, size), :] = row_ops[
                last - 1 + place, pl.ds(half * size, size), (2 - place) * size:(3 - place) * size]

    def tend(step):
        @pl.when(step + AHEAD < last)
        def _():
            send(step + AHEAD)

        for at in (step, chunks - 1 - step):
            keep(at + 1, smooth(at))
        finish(step - 1)
        finish(chunks - step)

    @pl.loop(2, last - 3)
    def _(step):
        tend(step)

    for side, turn in ((0, jnp.logical_not(odd)), (1, odd)):
        @pl.when(relays & turn)
        def _():
            first_leg(side).wait_recv()
            second_leg(side).start()

    @pl.loop(last - 3, last - 1)
    def _(step):
        tend(step)

    @pl.when(has_up)
    def _():
        down.wait_recv()
        keep(0, edge_in[0])

    @pl.when(has_down)
    def _():
        up.wait_recv()
        keep(chunks + 1, edge_in[1])

    @pl.when(jnp.logical_not(has_up))
    def _():
        keep(0, jnp.zeros((size, width), F32))

    @pl.when(jnp.logical_not(has_down))
    def _():
        keep(chunks + 1, jnp.zeros((size, width), F32))

    finish(0)
    finish(chunks - 1)
    keep(last, smooth(last - 1))
    ready = blend(1, own, last)
    for at in (last - 2, last + 1, last - 1, last):
        finish(at)

    arrive(last)
    high, low = split(across(ready + blend(0, left_in, last) + blend(2, right_in, last)))
    three = 3 * size
    both = dot(tail_op[...], high)
    share = both[:three] + both[three:] + dot(tail_op[:three, :], low)
    for place in range(3):
        out[last - 1 + place] += share[place * size:(place + 1) * size]

    for side, turn in ((0, jnp.logical_not(odd)), (1, odd)):
        @pl.when(relays & turn)
        def _():
            second_leg(side).wait_send()

    @pl.when(has_up)
    def _():
        up.wait_send()

    @pl.when(has_down)
    def _():
        down.wait_send()

    @pl.loop(0, chunks)
    def _(at):
        @pl.when(has_right)
        def _():
            to_right(at).wait_send()

        @pl.when(has_left)
        def _():
            to_left(at).wait_send()


def solution(mesh):
    groups, skies = mesh.shape["chan"], mesh.shape["sky"]

    def per_device(cube, shifts, halfwidth, taps, beam_rows, beam_cols):
        height, chans, width = cube.shape
        chunks, size = height // BAND, BAND * chans
        stay = pl.BlockSpec(memory_space=pltpu.HBM)
        whole = (chunks, size, width)
        result = pl.pallas_call(
            functools.partial(kernel, groups, skies),
            out_shape=pltpu.VMEM(whole, F32),
            in_specs=[stay] * 6,
            out_specs=pl.BlockSpec(memory_space=pltpu.VMEM),
            scratch_shapes=[
                pltpu.SMEM(shifts.shape, jnp.int32),
                pltpu.SMEM(halfwidth.shape, jnp.int32),
                pltpu.VMEM(taps.shape, F32),
                pltpu.VMEM(whole, F32),
                pltpu.VMEM(whole, F32),
                pltpu.VMEM(whole, F32),
                pltpu.VMEM((chunks + 2, size, width), BF16),
                pltpu.VMEM((chunks + 2, size, width), BF16),
                pltpu.VMEM((6 * size, size), BF16),
                pltpu.VMEM((2, size, width), F32),
                pltpu.VMEM((2, size, width), F32),
                pltpu.VMEM((size, width), F32),
                pltpu.VMEM((width, width), F32),
                pltpu.VMEM((2, width, width), BF16),
                pltpu.VMEM((height, 3 * height), F32),
                pltpu.VMEM((chunks, 2 * size, 3 * size), BF16),
                pltpu.VMEM((2 * size, 3 * size), BF16),
                pltpu.SemaphoreType.DMA((8,)),
                pltpu.SemaphoreType.DMA((2, chunks)),
                pltpu.SemaphoreType.DMA((2, chunks)),
                pltpu.SemaphoreType.DMA((3,)),
                pltpu.SemaphoreType.DMA((3,)),
            ],
            compiler_params=pltpu.CompilerParams(collective_id=0, has_side_effects=True, vmem_limit_bytes=48 << 20),
            name="regrid",
        )(*(pltpu.with_memory_space_constraint(x, pltpu.HBM) for x in (
            cube.reshape(whole), shifts, halfwidth, taps, beam_rows, beam_cols)))
        return result.reshape(cube.shape)

    return jax.shard_map(
        per_device,
        mesh=mesh,
        in_specs=(P("sky", "chan", None), P("chan"), P("chan"), P("chan", None), P(), P()),
        out_specs=P("sky", "chan", None),
        check_vma=False,
    )
```

```python
import functools

import jax
import jax.numpy as jnp
from jax import lax
from jax.experimental import pallas as pl
from jax.experimental.pallas import tpu as pltpu
from jax.sharding import PartitionSpec as P

BLK = 4
S_MAX = 12
RADIUS = 4
BAND = 8
SLOTS = 12
AHEAD = 2
RUN = 4
INNER = 8
MESH = pl.DeviceIdType.MESH
BF16 = jnp.bfloat16
F32 = jnp.float32
ACROSS = (((1,), (1,)), ((), ()))


def split(x):
    high = x.astype(BF16)
    return high, (x - high.astype(F32)).astype(BF16)


def dot(a, b):
    return jnp.dot(a, b, preferred_element_type=F32)


def dot_across(a, b):
    return lax.dot_general(a, b, ACROSS, preferred_element_type=F32)


def iota(shape, dim):
    return lax.broadcasted_iota(jnp.int32, shape, dim)


def ones_where(condition):
    return jnp.where(condition, 1.0, 0.0).astype(BF16)


def deepen(x):
    return jnp.concatenate([x, jnp.zeros((128 - x.shape[0], x.shape[1]), x.dtype)], axis=0)


def need(band):
    shape = band.shape
    row, lane = iota(shape, 0), iota(shape, 1)
    ones, before = jnp.ones((128, 128), BF16), ones_where(iota((128, 128), 0) < iota((128, 128), 1))
    pattern = ones_where(band != 0.0)
    high, low = split(band)
    touched = ones_where(dot_across(ones[:shape[0]], deepen(pattern)) > 0.5)
    few_out = dot(touched, ones)
    pick = ones_where((dot(touched, before).astype(jnp.int32) == row) & (touched > 0.5))
    send_out = dot(pick, deepen(high)) + dot(pick, deepen(low))
    touched = ones_where(dot(pattern, ones) > 0.5)
    rank = dot(ones_where(lane < row), deepen(touched)).astype(jnp.int32)
    receive_out = jnp.where((rank == lane) & (touched > 0.5), 1.0, 0.0)
    touched = ones_where(dot(ones[:shape[0]], deepen(pattern)) > 0.5)
    few_raw = dot(touched, ones)
    pick = ones_where((dot(touched, before).astype(jnp.int32) == row) & (touched > 0.5))
    outs = few_out <= few_raw
    send = jnp.where(outs, send_out, pick.astype(F32))
    high = jnp.where(outs, receive_out, dot_across(high, deepen(pick)))
    low = jnp.where(outs, 0.0, dot_across(low, deepen(pick)))
    return send, (high.astype(BF16), low.astype(BF16)), jnp.minimum(few_out, few_raw)


def kernel(lean, groups, skies, *refs):
    cube, shifts_in, halfwidth_in, taps_in, beam_rows, beam_cols, out, *refs = refs
    if lean:
        flag, needs, asked, for_left, for_right, send_ops, receive_ops, near_flags, far_flags, my_flag, *refs = refs
        need_send, need_recv, flag_send, flag_recv, *refs = refs
    (shifts, halfwidth, taps, own, left_in, right_in, spread, spread_low, tail_op, edge_out, edge_in, detour, cols,
     cols_pair, rows, row_ops, chan_op, local_sem, send_sem, recv_sem, edge_send, edge_recv) = refs
    chunks, size, width = cube.shape
    chans = size // BAND
    reach = S_MAX + RADIUS
    thin = SLOTS * BAND
    last = chunks // 2
    group, sky = lax.axis_index("chan"), lax.axis_index("sky")
    has_left, has_right = group > 0, group < groups - 1
    has_up, has_down = sky > 0, sky < skies - 1
    inner = min(INNER, groups)
    outer = groups // inner
    at_inner, at_outer = lax.rem(group, inner), group // inner
    spot = lax.rem(group, RUN)
    odd = lax.rem(sky, 2) == 1
    crosses = jnp.where(odd, has_down, has_up)
    beyond = jnp.where(odd, sky + 1, sky - 1)
    beside = jnp.where(spot == 0, group + 1, group - 1)
    detours = crosses & ((spot == 0) | (spot == RUN - 1)) & (beside < groups)
    served = jnp.where(spot == 1, group - 1, group + 1)
    relays = crosses & ((spot == 1) | (spot == RUN - 2)) & (served < groups)

    barrier = pltpu.get_barrier_semaphore()
    sides = [(has_left, {"chan": group - 1}), (has_right, {"chan": group + 1}),
             (has_up, {"sky": sky - 1}), (has_down, {"sky": sky + 1})]
    near = [(at_inner != peer, {"chan": at_outer * inner + peer}) for peer in range(inner)] if lean else []
    far = [(at_outer != peer, {"chan": peer * inner + at_inner}) for peer in range(outer)] if lean else []
    waits = relays.astype(jnp.int32)
    for there, device in sides + near + far:
        @pl.when(there)
        def _():
            pl.semaphore_signal(barrier, inc=1, device_id=device, device_id_type=MESH)

        waits = waits + there.astype(jnp.int32)

    @pl.when(detours)
    def _():
        pl.semaphore_signal(barrier, inc=1, device_id={"chan": beside, "sky": beyond}, device_id_type=MESH)

    height = chunks * BAND
    local = [
        pltpu.make_async_copy(shifts_in, shifts, local_sem.at[5]),
        pltpu.make_async_copy(halfwidth_in, halfwidth, local_sem.at[6]),
        pltpu.make_async_copy(taps_in, taps, local_sem.at[7]),
        pltpu.make_async_copy(cube, own, local_sem.at[0]),
        pltpu.make_async_copy(beam_cols, cols, local_sem.at[1]),
    ]
    for part in range(3):
        block = lax.rem(sky + skies + part - 1, skies)
        local.append(pltpu.make_async_copy(
            beam_rows.at[pl.ds(pl.multiple_of(sky * height, height), height),
                         pl.ds(pl.multiple_of(block * height, height), height)],
            rows.at[:, pl.ds(part * height, height)], local_sem.at[2 + part]))
    for copy in local:
        copy.start()
    for copy in local[:3]:
        copy.wait()

    chan = iota((chans, 128), 0)
    place = iota((chans, 128), 1)
    offsets = jnp.zeros((chans, 128), jnp.int32)
    limits = jnp.zeros((chans, 2 * RADIUS + 1), jnp.int32)
    for block in range(chans // BLK):
        offsets = jnp.where(chan // BLK == block, shifts[block], offsets)
        limits = jnp.where(iota(limits.shape, 0) // BLK == block, halfwidth[block], limits)
    masked = jnp.where(jnp.abs(iota(limits.shape, 1) - RADIUS) <= limits, taps[...], 0.0)
    weights = masked / jnp.sum(masked, axis=1, keepdims=True)

    def slab(base):
        band = jnp.zeros((chans, 128), F32)
        for tap in range(2 * RADIUS + 1):
            spot = chan + reach + offsets + (tap - RADIUS) - base
            band = band + jnp.where((place == spot) & (place < chans), weights[:, tap:tap + 1], 0.0)
        return band

    left_band = jnp.where(has_left, slab(0), 0.0)
    right_band = jnp.where(has_right, slab(2 * chans), 0.0)
    bands = (left_band, slab(chans), right_band)

    if lean:
        receives = []
        over = jnp.zeros((chans, 128), F32)
        for side, band in enumerate((bands[0], bands[2])):
            send, receive, count = need(band)
            needs[side] = send
            receives.append(receive)
            over = over + jnp.where(count > SLOTS + 0.5, 1.0, 0.0)
        my_flag[0] = over[:8]
        near_flags[at_inner] = over[:8]

        @pl.when(jnp.logical_not(has_left))
        def _():
            asked[0] = jnp.zeros((chans, 128), F32)

        @pl.when(jnp.logical_not(has_right))
        def _():
            asked[1] = jnp.zeros((chans, 128), F32)

    pl.semaphore_wait(barrier, waits)

    def thinned(ref, at, raw):
        return ref.at[at] if raw else ref.at[at, pl.ds(0, thin)]

    def to_right(at, raw):
        return pltpu.make_async_remote_copy(
            src_ref=cube.at[at] if raw else for_right.at[at], dst_ref=thinned(left_in, at, raw),
            send_sem=send_sem.at[0, at], recv_sem=recv_sem.at[0, at],
            device_id={"chan": group + 1}, device_id_type=MESH)

    def to_left(at, raw):
        return pltpu.make_async_remote_copy(
            src_ref=cube.at[at] if raw else for_left.at[at], dst_ref=thinned(right_in, at, raw),
            send_sem=send_sem.at[1, at], recv_sem=recv_sem.at[1, at],
            device_id={"chan": group - 1}, device_id_type=MESH)

    def send(step, raw):
        for at in (step, chunks - 1 - step):
            @pl.when(has_right)
            def _():
                to_right(at, raw).start()

            @pl.when(has_left)
            def _():
                to_left(at, raw).start()

    def ask(side):
        return pltpu.make_async_remote_copy(
            src_ref=needs.at[side], dst_ref=asked.at[1 - side], send_sem=need_send.at[side],
            recv_sem=need_recv.at[1 - side], device_id=sides[side][1], device_id_type=MESH)

    def tell(stage, peer):
        target, mine = ((near_flags, at_inner), (far_flags, at_outer))[stage]
        return pltpu.make_async_remote_copy(
            src_ref=my_flag.at[stage], dst_ref=target.at[mine], send_sem=flag_send.at[stage, peer],
            recv_sem=flag_recv.at[stage, mine], device_id=(near, far)[stage][peer][1], device_id_type=MESH)

    def told(stage, peer):
        source = (near_flags, far_flags)[stage].at[peer]
        return pltpu.make_async_remote_copy(
            src_ref=my_flag.at[stage], dst_ref=source, send_sem=flag_send.at[stage, peer],
            recv_sem=flag_recv.at[stage, peer], device_id=(near, far)[stage][peer][1], device_id_type=MESH)

    def each(stage, act):
        for peer, (there, _) in enumerate((near, far)[stage]):
            @pl.when(there)
            def _():
                act(peer)

    if lean:
        for side in range(2):
            @pl.when(sides[side][0])
            def _():
                ask(side).start()

        each(0, lambda peer: tell(0, peer).start())

    send(0, True)
    if not lean:
        send(1, True)

    @pl.when(jnp.logical_not(has_left))
    def _():
        left_in[...] = jnp.zeros(left_in.shape, F32)

    @pl.when(jnp.logical_not(has_right))
    def _():
        right_in[...] = jnp.zeros(right_in.shape, F32)

    for copy in local[3:]:
        copy.wait()

    def apply(op, value, rows_out):
        high, low = split(value)
        both = dot(op, high)
        return both[:rows_out] + both[rows_out:] + dot(op[:rows_out], low)

    def reduce_for(step):
        for at in (step, chunks - 1 - step):
            for side, ref in enumerate((for_left, for_right)):
                ref[at] = apply(send_ops[side], own[at], thin)

    if lean:
        for side in range(2):
            @pl.when(sides[side][0])
            def _():
                ask(1 - side).wait_recv()

        pick = ones_where(iota((128, 128), 0) == iota((128, 128), 1) % chans)
        same_row = iota((128, 128), 0) % BAND == iota((128, 128), 1) // chans
        for side in range(2):
            for half, part in enumerate(split(asked[side])):
                wide = jnp.broadcast_to(dot(part, pick)[:, None, :], (chans, BAND, 128)).reshape(128, 128)
                send_ops[side, pl.ds(half * thin, thin), :] = jnp.where(same_row, wide, 0.0)[:thin].astype(BF16)
        reduce_for(1)

    pick = ones_where(iota((128, size), 0) == iota((128, size), 1) % chans)
    same_row = iota((size, size), 0) // chans == iota((size, size), 1) // chans
    for slot, band in enumerate(bands):
        for half, part in enumerate(split(band)):
            wide = jnp.concatenate([dot(part, pick)] * BAND, axis=0)
            chan_op[pl.ds(half * size, size), pl.ds(slot * size, size)] = jnp.where(same_row, wide, 0.0).astype(BF16)
    if lean:
        send(1, False)
        pick = ones_where(iota((128, 128), 0) == iota((128, 128), 1) // BAND)
        same_row = iota((size, 128), 0) // chans == iota((size, 128), 1) % BAND
        for side, receive in enumerate(receives):
            for half, part in enumerate(receive):
                wide = jnp.concatenate([dot(part, pick)] * BAND, axis=0)
                receive_ops[side, pl.ds(half * size, size), :] = jnp.where(same_row, wide, 0.0).astype(BF16)
        reduce_for(2)

    high, low = split(cols[...])
    cols_pair[0] = high
    cols_pair[1] = low

    pick = ones_where(iota((128, 3 * size), 0) == iota((128, 3 * size), 1) // chans)
    same_chan = iota((size, 3 * size), 0) % chans == iota((size, 3 * size), 1) % chans
    for at in range(chunks):
        start = height + (at - 1) * BAND
        close = rows[pl.ds(at * BAND, BAND), start:start + 3 * BAND]
        close = jnp.concatenate([close, jnp.zeros((BAND, 128 - 3 * BAND), F32)], axis=1)
        for half, part in enumerate(split(close)):
            wide = dot(part, pick)
            wide = jnp.broadcast_to(wide[:, None, :], (BAND, chans, 3 * size)).reshape(size, 3 * size)
            row_ops[at, pl.ds(half * size, size), :] = jnp.where(same_chan, wide, 0.0).astype(BF16)

    def keep(at, value):
        high, low = split(value)
        spread[at] = high
        spread_low[at] = low

    def arrive(at, raw):
        @pl.when(has_left)
        def _():
            to_right(at, raw).wait_recv()

        @pl.when(has_right)
        def _():
            to_left(at, raw).wait_recv()

    def blend(part, ref, at, raw=True):
        if raw:
            return apply(chan_op[:, part * size:(part + 1) * size], ref[at], size)
        return apply(receive_ops[part // 2, :, :thin], ref[at, pl.ds(0, thin)], size)

    def across(total):
        high, low = split(total)
        both = dot_across(jnp.concatenate([high, low], axis=0), cols_pair[0])
        return both[:size] + both[size:] + dot_across(high, cols_pair[1])

    def smooth(at, raw):
        arrive(at, raw)
        return across(blend(1, own, at) + blend(0, left_in, at, raw) + blend(2, right_in, at, raw))

    def finish(at):
        op = row_ops[at]
        both = dot(op, spread[pl.ds(at, 3)].reshape(3 * size, width))
        out[at] = both[:size] + both[size:] + dot(op[:size], spread_low[pl.ds(at, 3)].reshape(3 * size, width))

    whole = not lean
    for side, at in enumerate((0, chunks - 1)):
        value = smooth(at, True)
        edge_out[side] = value
        keep(at + 1, value)
    if lean:
        each(0, lambda peer: told(0, peer).wait_recv())
        total = near_flags[0]
        for peer in range(1, inner):
            total = total + near_flags[peer]
        my_flag[1] = total
        far_flags[at_outer] = total

    def edge(side, device):
        return pltpu.make_async_remote_copy(
            src_ref=edge_out.at[side], dst_ref=edge_in.at[1 - side], send_sem=edge_send.at[side],
            recv_sem=edge_recv.at[1 - side], device_id=device, device_id_type=MESH)

    up, down = edge(0, {"sky": sky - 1}), edge(1, {"sky": sky + 1})

    def first_leg(side):
        return pltpu.make_async_remote_copy(
            src_ref=edge_out.at[side], dst_ref=detour, send_sem=edge_send.at[side], recv_sem=edge_recv.at[2],
            device_id={"chan": beside}, device_id_type=MESH)

    def second_leg(side):
        return pltpu.make_async_remote_copy(
            src_ref=detour, dst_ref=edge_in.at[1 - side], send_sem=edge_send.at[2],
            recv_sem=edge_recv.at[1 - side], device_id={"chan": served, "sky": beyond}, device_id_type=MESH)

    turns = ((0, jnp.logical_not(odd)), (1, odd))
    for side, turn in turns:
        there, copy = ((has_up, up), (has_down, down))[side]

        @pl.when(there & jnp.logical_not(detours & turn))
        def _():
            copy.start()

        @pl.when(detours & turn)
        def _():
            first_leg(side).start()

    for step in range(2, AHEAD + 2):
        send(step, whole)
        if lean:
            reduce_for(step + 1)
    for at in (1, chunks - 2):
        keep(at + 1, smooth(at, whole))
    if lean:
        each(1, lambda peer: tell(1, peer).start())

    keep(last + 1, jnp.zeros((size, width), F32))
    for spot in range(3):
        for half in range(2):
            tail_op[pl.ds((3 * half + spot) * size, size), :] = row_ops[
                last - 1 + spot, pl.ds(half * size, size), (2 - spot) * size:(3 - spot) * size]

    def tend(step):
        @pl.when(step + AHEAD < last)
        def _():
            send(step + AHEAD, whole)

        if lean:
            @pl.when(step + AHEAD + 1 < last)
            def _():
                reduce_for(step + AHEAD + 1)

        for at in (step, chunks - 1 - step):
            keep(at + 1, smooth(at, whole))
        finish(step - 1)
        finish(chunks - step)

    @pl.loop(2, last - 3)
    def _(step):
        tend(step)

    for side, turn in turns:
        @pl.when(relays & turn)
        def _():
            first_leg(side).wait_recv()
            second_leg(side).start()

    if lean:
        each(1, lambda peer: told(1, peer).wait_recv())
        total = far_flags[0]
        for peer in range(1, outer):
            total = total + far_flags[peer]
        flag[...] = total

    @pl.loop(last - 3, last - 1)
    def _(step):
        tend(step)

    @pl.when(has_up)
    def _():
        down.wait_recv()
        keep(0, edge_in[0])

    @pl.when(has_down)
    def _():
        up.wait_recv()
        keep(chunks + 1, edge_in[1])

    @pl.when(jnp.logical_not(has_up))
    def _():
        keep(0, jnp.zeros((size, width), F32))

    @pl.when(jnp.logical_not(has_down))
    def _():
        keep(chunks + 1, jnp.zeros((size, width), F32))

    finish(0)
    finish(chunks - 1)
    keep(last, smooth(last - 1, whole))
    ready = blend(1, own, last)
    for at in (last - 2, last + 1, last - 1, last):
        finish(at)

    arrive(last, whole)
    high, low = split(across(ready + blend(0, left_in, last, whole) + blend(2, right_in, last, whole)))
    three = 3 * size
    both = dot(tail_op[...], high)
    share = both[:three] + both[three:] + dot(tail_op[:three, :], low)
    for spot in range(3):
        out[last - 1 + spot] += share[spot * size:(spot + 1) * size]

    for side, turn in turns:
        @pl.when(relays & turn)
        def _():
            second_leg(side).wait_send()

    for (there, _), wait in zip(sides[2:], (up, down)):
        @pl.when(there)
        def _():
            wait.wait_send()

    if lean:
        for side in range(2):
            @pl.when(sides[side][0])
            def _():
                ask(side).wait_send()

        each(0, lambda peer: tell(0, peer).wait_send())
        each(1, lambda peer: tell(1, peer).wait_send())

    def sent(at, raw):
        @pl.when(has_right)
        def _():
            to_right(at, raw).wait_send()

        @pl.when(has_left)
        def _():
            to_left(at, raw).wait_send()

    sent(0, True)
    sent(chunks - 1, True)

    @pl.loop(1, chunks - 1)
    def _(at):
        sent(at, whole)


def store(x):
    pieces = 4

    def body(x_ref, out_ref, sem):
        step = x.shape[0] // pieces
        copies = [pltpu.make_async_copy(x_ref.at[pl.ds(at * step, step)], out_ref.at[pl.ds(at * step, step)], sem.at[at])
                  for at in range(pieces)]
        for copy in copies:
            copy.start()
        for copy in copies:
            copy.wait()

    return pl.pallas_call(
        body, out_shape=pltpu.HBM(x.shape, x.dtype), in_specs=[pl.BlockSpec(memory_space=pltpu.VMEM)],
        out_specs=pl.BlockSpec(memory_space=pltpu.HBM), scratch_shapes=[pltpu.SemaphoreType.DMA((pieces,))],
        compiler_params=pltpu.CompilerParams(vmem_limit_bytes=1 << 20), name="store",
    )(pltpu.with_memory_space_constraint(x, pltpu.VMEM))


def solution(mesh):
    groups, skies = mesh.shape["chan"], mesh.shape["sky"]

    def regrid(lean, cube, shifts, halfwidth, taps, beam_rows, beam_cols):
        chunks, size, width = cube.shape
        height, chans = chunks * BAND, size // BAND
        thin = SLOTS * BAND
        inner = min(INNER, groups)
        outer = groups // inner
        whole = (chunks, size, width)
        vmem = pl.BlockSpec(memory_space=pltpu.VMEM)
        results, extra = [pltpu.VMEM(whole, F32)], []
        if lean:
            results.append(jax.ShapeDtypeStruct((8, 128), F32))
            extra = [
                pltpu.VMEM((2, chans, 128), F32),
                pltpu.VMEM((2, chans, 128), F32),
                pltpu.VMEM((chunks, thin, width), F32),
                pltpu.VMEM((chunks, thin, width), F32),
                pltpu.VMEM((2, 2 * thin, 128), BF16),
                pltpu.VMEM((2, 2 * size, 128), BF16),
                pltpu.VMEM((inner, 8, 128), F32),
                pltpu.VMEM((outer, 8, 128), F32),
                pltpu.VMEM((2, 8, 128), F32),
                pltpu.SemaphoreType.DMA((2,)),
                pltpu.SemaphoreType.DMA((2,)),
                pltpu.SemaphoreType.DMA((2, max(inner, outer))),
                pltpu.SemaphoreType.DMA((2, max(inner, outer))),
            ]
        return pl.pallas_call(
            functools.partial(kernel, lean, groups, skies),
            out_shape=results,
            in_specs=[pl.BlockSpec(memory_space=pltpu.HBM)] * 6,
            out_specs=[vmem] * len(results),
            scratch_shapes=extra + [
                pltpu.SMEM(shifts.shape, jnp.int32),
                pltpu.SMEM(halfwidth.shape, jnp.int32),
                pltpu.VMEM(taps.shape, F32),
                pltpu.VMEM(whole, F32),
                pltpu.VMEM(whole, F32),
                pltpu.VMEM(whole, F32),
                pltpu.VMEM((chunks + 2, size, width), BF16),
                pltpu.VMEM((chunks + 2, size, width), BF16),
                pltpu.VMEM((6 * size, size), BF16),
                pltpu.VMEM((2, size, width), F32),
                pltpu.VMEM((2, size, width), F32),
                pltpu.VMEM((size, width), F32),
                pltpu.VMEM((width, width), F32),
                pltpu.VMEM((2, width, width), BF16),
                pltpu.VMEM((height, 3 * height), F32),
                pltpu.VMEM((chunks, 2 * size, 3 * size), BF16),
                pltpu.VMEM((2 * size, 3 * size), BF16),
                pltpu.SemaphoreType.DMA((8,)),
                pltpu.SemaphoreType.DMA((2, chunks)),
                pltpu.SemaphoreType.DMA((2, chunks)),
                pltpu.SemaphoreType.DMA((3,)),
                pltpu.SemaphoreType.DMA((3,)),
            ],
            compiler_params=pltpu.CompilerParams(
                collective_id=int(lean), has_side_effects=True, vmem_limit_bytes=40 << 20),
            name="regrid" if lean else "regrid_whole",
        )(*(pltpu.with_memory_space_constraint(x, pltpu.HBM) for x in (
            cube, shifts, halfwidth, taps, beam_rows, beam_cols)))

    def per_device(cube, *others):
        height, chans, width = cube.shape
        args = (cube.reshape(height // BAND, BAND * chans, width), *others)
        result, flag = regrid(True, *args)
        result, _ = lax.while_loop(
            lambda state: state[1] > 0.5,
            lambda state: (store(regrid(False, *args)[0]), jnp.zeros((), F32)),
            (store(result), flag[0, 0]))
        return result.reshape(cube.shape)

    return jax.shard_map(
        per_device,
        mesh=mesh,
        in_specs=(P("sky", "chan", None), P("chan"), P("chan"), P("chan", None), P(), P()),
        out_specs=P("sky", "chan", None),
        check_vma=False,
    )
```

```python
import functools

import jax
import jax.numpy as jnp
from jax import lax
from jax.experimental import pallas as pl
from jax.experimental.pallas import tpu as pltpu
from jax.sharding import PartitionSpec as P

BLK = 4
S_MAX = 12
RADIUS = 4
BAND = 8
SLOTS = 12
AHEAD = 2
RUN = 4
INNER = 8
MESH = pl.DeviceIdType.MESH
BF16 = jnp.bfloat16
F32 = jnp.float32
ACROSS = (((1,), (1,)), ((), ()))


def split(x):
    high = x.astype(BF16)
    return high, (x - high.astype(F32)).astype(BF16)


def dot(a, b):
    return jnp.dot(a, b, preferred_element_type=F32)


def dot_across(a, b):
    return lax.dot_general(a, b, ACROSS, preferred_element_type=F32)


def iota(shape, dim):
    return lax.broadcasted_iota(jnp.int32, shape, dim)


def ones_where(condition):
    return jnp.where(condition, 1.0, 0.0).astype(BF16)


def deepen(x):
    return jnp.concatenate([x, jnp.zeros((128 - x.shape[0], x.shape[1]), x.dtype)], axis=0)


def need(band):
    shape = band.shape
    row, lane = iota(shape, 0), iota(shape, 1)
    ones, before = jnp.ones((128, 128), BF16), ones_where(iota((128, 128), 0) < iota((128, 128), 1))
    one_rows = ones[:shape[0]]
    pattern = ones_where(band != 0.0)
    high, low = split(band)
    raw = jnp.zeros(shape, F32)
    for block in range(shape[0] // BLK):
        raw = jnp.where(lane // BLK == block, (row // 2 ** block % 2).astype(F32), raw)
    touched = jnp.where(dot_across(one_rows, deepen(pattern)) > 0.5, 1.0, 0.0)
    channels = ones_where(dot(raw.astype(BF16), deepen(pattern)) > 0.5)
    cost = dot(channels, ones) + dot((touched * (1.0 - raw)).astype(BF16), ones)
    score = cost * shape[0] + row.astype(F32)
    best = jnp.min(score, axis=0, keepdims=True)
    chosen = jnp.sum(jnp.where(score == best, raw, 0.0), axis=0, keepdims=True)
    raw = dot(ones_where((row == lane) & (chosen > 0.5)), ones)
    pattern_raw = (pattern.astype(F32) * raw).astype(BF16)
    pattern_out = (pattern.astype(F32) * (1.0 - raw)).astype(BF16)
    hit = ones_where(dot(one_rows, deepen(pattern_raw)) > 0.5)
    channels = dot(hit, ones)
    pick_raw = ones_where((dot(hit, before) == row.astype(F32)) & (hit > 0.5))
    hit = ones_where(dot_across(one_rows, deepen(pattern_out)) > 0.5)
    count = channels + dot(hit, ones)
    pick_out = ones_where((channels + dot(hit, before) == row.astype(F32)) & (hit > 0.5))
    send = pick_raw.astype(F32) + (dot(pick_out, deepen(high)) + dot(pick_out, deepen(low)))
    hit = ones_where(dot(pattern_out, ones) > 0.5)
    place = channels + dot(ones_where(lane < row), deepen(hit))
    receive_out = jnp.where((place == lane.astype(F32)) & (hit > 0.5), 1.0, 0.0)
    high_raw = dot_across((high.astype(F32) * raw).astype(BF16), deepen(pick_raw))
    low_raw = dot_across((low.astype(F32) * raw).astype(BF16), deepen(pick_raw))
    return send, ((receive_out + high_raw).astype(BF16), low_raw.astype(BF16)), count


def kernel(lean, groups, skies, *refs):
    cube, shifts_in, halfwidth_in, taps_in, beam_rows, beam_cols, out, *refs = refs
    if lean:
        flag, needs, asked, for_both, send_op, receive_ops, near_flags, far_flags, my_flag, *refs = refs
        need_send, need_recv, flag_send, flag_recv, *refs = refs
    (shifts, halfwidth, taps, own, left_in, right_in, spread, spread_low, tail_op, edge_out, edge_in, detour, cols,
     cols_pair, rows, row_ops, chan_op, local_sem, send_sem, recv_sem, edge_send, edge_recv) = refs
    chunks, size, width = cube.shape
    chans = size // BAND
    reach = S_MAX + RADIUS
    thin = SLOTS * BAND
    last = chunks // 2
    group, sky = lax.axis_index("chan"), lax.axis_index("sky")
    has_left, has_right = group > 0, group < groups - 1
    has_up, has_down = sky > 0, sky < skies - 1
    inner = min(INNER, groups)
    outer = groups // inner
    at_inner, at_outer = lax.rem(group, inner), group // inner
    spot = lax.rem(group, RUN)
    odd = lax.rem(sky, 2) == 1
    crosses = jnp.where(odd, has_down, has_up)
    beyond = jnp.where(odd, sky + 1, sky - 1)
    beside = jnp.where(spot == 0, group + 1, group - 1)
    detours = crosses & ((spot == 0) | (spot == RUN - 1)) & (beside < groups)
    served = jnp.where(spot == 1, group - 1, group + 1)
    relays = crosses & ((spot == 1) | (spot == RUN - 2)) & (served < groups)

    barrier = pltpu.get_barrier_semaphore()
    sides = [(has_left, {"chan": group - 1}), (has_right, {"chan": group + 1}),
             (has_up, {"sky": sky - 1}), (has_down, {"sky": sky + 1})]
    near = [(at_inner != peer, {"chan": at_outer * inner + peer}) for peer in range(inner)] if lean else []
    far = [(at_outer != peer, {"chan": peer * inner + at_inner}) for peer in range(outer)] if lean else []
    waits = relays.astype(jnp.int32)
    for there, device in sides + near + far:
        @pl.when(there)
        def _():
            pl.semaphore_signal(barrier, inc=1, device_id=device, device_id_type=MESH)

        waits = waits + there.astype(jnp.int32)

    @pl.when(detours)
    def _():
        pl.semaphore_signal(barrier, inc=1, device_id={"chan": beside, "sky": beyond}, device_id_type=MESH)

    height = chunks * BAND
    local = [
        pltpu.make_async_copy(shifts_in, shifts, local_sem.at[5]),
        pltpu.make_async_copy(halfwidth_in, halfwidth, local_sem.at[6]),
        pltpu.make_async_copy(taps_in, taps, local_sem.at[7]),
        pltpu.make_async_copy(cube, own, local_sem.at[0]),
        pltpu.make_async_copy(beam_cols, cols, local_sem.at[1]),
    ]
    for part in range(3):
        block = lax.rem(sky + skies + part - 1, skies)
        local.append(pltpu.make_async_copy(
            beam_rows.at[pl.ds(pl.multiple_of(sky * height, height), height),
                         pl.ds(pl.multiple_of(block * height, height), height)],
            rows.at[:, pl.ds(part * height, height)], local_sem.at[2 + part]))
    for copy in local:
        copy.start()
    for copy in local[:3]:
        copy.wait()

    chan = iota((chans, 128), 0)
    place = iota((chans, 128), 1)
    offsets = jnp.zeros((chans, 128), jnp.int32)
    limits = jnp.zeros((chans, 2 * RADIUS + 1), jnp.int32)
    for block in range(chans // BLK):
        offsets = jnp.where(chan // BLK == block, shifts[block], offsets)
        limits = jnp.where(iota(limits.shape, 0) // BLK == block, halfwidth[block], limits)
    masked = jnp.where(jnp.abs(iota(limits.shape, 1) - RADIUS) <= limits, taps[...], 0.0)
    weights = masked / jnp.sum(masked, axis=1, keepdims=True)

    def slab(base):
        band = jnp.zeros((chans, 128), F32)
        for tap in range(2 * RADIUS + 1):
            spot = chan + reach + offsets + (tap - RADIUS) - base
            band = band + jnp.where((place == spot) & (place < chans), weights[:, tap:tap + 1], 0.0)
        return band

    left_band = jnp.where(has_left, slab(0), 0.0)
    right_band = jnp.where(has_right, slab(2 * chans), 0.0)
    bands = (left_band, slab(chans), right_band)

    if lean:
        receives = []
        over = jnp.zeros((chans, 128), F32)
        for side, band in enumerate((bands[0], bands[2])):
            send, receive, count = need(band)
            needs[side] = send
            receives.append(receive)
            over = over + jnp.where(count > SLOTS + 0.5, 1.0, 0.0)
        my_flag[0] = over[:8]
        near_flags[at_inner] = over[:8]

        @pl.when(jnp.logical_not(has_left))
        def _():
            asked[0] = jnp.zeros((chans, 128), F32)

        @pl.when(jnp.logical_not(has_right))
        def _():
            asked[1] = jnp.zeros((chans, 128), F32)

    pl.semaphore_wait(barrier, waits)

    def thinned(ref, at, raw):
        return ref.at[at] if raw else ref.at[at, pl.ds(0, thin)]

    def to_right(at, raw):
        return pltpu.make_async_remote_copy(
            src_ref=cube.at[at] if raw else for_both.at[at, pl.ds(thin, thin)], dst_ref=thinned(left_in, at, raw),
            send_sem=send_sem.at[0, at], recv_sem=recv_sem.at[0, at],
            device_id={"chan": group + 1}, device_id_type=MESH)

    def to_left(at, raw):
        return pltpu.make_async_remote_copy(
            src_ref=cube.at[at] if raw else for_both.at[at, pl.ds(0, thin)], dst_ref=thinned(right_in, at, raw),
            send_sem=send_sem.at[1, at], recv_sem=recv_sem.at[1, at],
            device_id={"chan": group - 1}, device_id_type=MESH)

    def send(at, raw):
        @pl.when(has_right)
        def _():
            to_right(at, raw).start()

        @pl.when(has_left)
        def _():
            to_left(at, raw).start()

    def send_pair(step, raw):
        send(step, raw)
        send(chunks - 1 - step, raw)

    def ask(side):
        return pltpu.make_async_remote_copy(
            src_ref=needs.at[side], dst_ref=asked.at[1 - side], send_sem=need_send.at[side],
            recv_sem=need_recv.at[1 - side], device_id=sides[side][1], device_id_type=MESH)

    def tell(stage, peer):
        target, mine = ((near_flags, at_inner), (far_flags, at_outer))[stage]
        return pltpu.make_async_remote_copy(
            src_ref=my_flag.at[stage], dst_ref=target.at[mine], send_sem=flag_send.at[stage, peer],
            recv_sem=flag_recv.at[stage, mine], device_id=(near, far)[stage][peer][1], device_id_type=MESH)

    def told(stage, peer):
        source = (near_flags, far_flags)[stage].at[peer]
        return pltpu.make_async_remote_copy(
            src_ref=my_flag.at[stage], dst_ref=source, send_sem=flag_send.at[stage, peer],
            recv_sem=flag_recv.at[stage, peer], device_id=(near, far)[stage][peer][1], device_id_type=MESH)

    def each(stage, act):
        for peer, (there, _) in enumerate((near, far)[stage]):
            @pl.when(there)
            def _():
                act(peer)

    if lean:
        for side in range(2):
            @pl.when(sides[side][0])
            def _():
                ask(side).start()

        each(0, lambda peer: tell(0, peer).start())

    send(0, True)
    if not lean:
        send(chunks - 1, True)
        send_pair(1, True)

    @pl.when(jnp.logical_not(has_left))
    def _():
        left_in[...] = jnp.zeros(left_in.shape, F32)

    @pl.when(jnp.logical_not(has_right))
    def _():
        right_in[...] = jnp.zeros(right_in.shape, F32)

    for copy in local[3:]:
        copy.wait()

    def apply(op, value, rows_out):
        high, low = split(value)
        both = dot(op, high)
        return both[:rows_out] + both[rows_out:] + dot(op[:rows_out], low)

    def reduce_for(at):
        for_both[at] = apply(send_op[...], own[at], 2 * thin)

    pick = ones_where(iota((128, size), 0) == iota((128, size), 1) % chans)
    same_row = iota((size, size), 0) // chans == iota((size, size), 1) // chans
    for slot, band in enumerate(bands):
        for half, part in enumerate(split(band)):
            wide = jnp.concatenate([dot(part, pick)] * BAND, axis=0)
            chan_op[pl.ds(half * size, size), pl.ds(slot * size, size)] = jnp.where(same_row, wide, 0.0).astype(BF16)
    if lean:
        pick = ones_where(iota((128, 128), 0) == iota((128, 128), 1) // BAND)
        same_row = iota((size, 128), 0) // chans == iota((size, 128), 1) % BAND
        for side, receive in enumerate(receives):
            for half, part in enumerate(receive):
                wide = jnp.concatenate([dot(part, pick)] * BAND, axis=0)
                receive_ops[side, pl.ds(half * size, size), :] = jnp.where(same_row, wide, 0.0).astype(BF16)

        for side in range(2):
            @pl.when(sides[side][0])
            def _():
                ask(1 - side).wait_recv()

        pick = ones_where(iota((128, 128), 0) == iota((128, 128), 1) % chans)
        same_row = iota((128, 128), 0) % BAND == iota((128, 128), 1) // chans
        for side in range(2):
            for half, part in enumerate(split(asked[side])):
                wide = jnp.broadcast_to(dot(part, pick)[:, None, :], (chans, BAND, 128)).reshape(128, 128)
                send_op[pl.ds((2 * half + side) * thin, thin), :] = jnp.where(same_row, wide, 0.0)[:thin].astype(BF16)
        reduce_for(chunks - 1)
        reduce_for(1)
        send(chunks - 1, False)
        reduce_for(chunks - 2)
        send(1, False)

    high, low = split(cols[...])
    cols_pair[0] = high
    cols_pair[1] = low

    pick = ones_where(iota((128, 3 * size), 0) == iota((128, 3 * size), 1) // chans)
    same_chan = iota((size, 3 * size), 0) % chans == iota((size, 3 * size), 1) % chans
    for at in range(chunks):
        start = height + (at - 1) * BAND
        close = rows[pl.ds(at * BAND, BAND), start:start + 3 * BAND]
        close = jnp.concatenate([close, jnp.zeros((BAND, 128 - 3 * BAND), F32)], axis=1)
        for half, part in enumerate(split(close)):
            wide = dot(part, pick)
            wide = jnp.broadcast_to(wide[:, None, :], (BAND, chans, 3 * size)).reshape(size, 3 * size)
            row_ops[at, pl.ds(half * size, size), :] = jnp.where(same_chan, wide, 0.0).astype(BF16)

    if lean:
        reduce_for(2)
        send(chunks - 2, False)

    def keep(at, value):
        high, low = split(value)
        spread[at] = high
        spread_low[at] = low

    def arrive(at, raw):
        @pl.when(has_left)
        def _():
            to_right(at, raw).wait_recv()

        @pl.when(has_right)
        def _():
            to_left(at, raw).wait_recv()

    def blend(part, ref, at, raw=True):
        if raw:
            return apply(chan_op[:, part * size:(part + 1) * size], ref[at], size)
        return apply(receive_ops[part // 2, :, :thin], ref[at, pl.ds(0, thin)], size)

    def across(total):
        high, low = split(total)
        both = dot_across(jnp.concatenate([high, low], axis=0), cols_pair[0])
        return both[:size] + both[size:] + dot_across(high, cols_pair[1])

    def smooth(at, raw):
        arrive(at, raw)
        return across(blend(1, own, at) + blend(0, left_in, at, raw) + blend(2, right_in, at, raw))

    def finish(at):
        op = row_ops[at]
        both = dot(op, spread[pl.ds(at, 3)].reshape(3 * size, width))
        out[at] = both[:size] + both[size:] + dot(op[:size], spread_low[pl.ds(at, 3)].reshape(3 * size, width))

    whole = not lean
    for side, at in enumerate((0, chunks - 1)):
        value = smooth(at, at == 0 or whole)
        edge_out[side] = value
        keep(at + 1, value)
        if lean:
            reduce_for((chunks - 3, 3)[side])
            send((2, chunks - 3)[side], False)
    if lean:
        each(0, lambda peer: told(0, peer).wait_recv())
        total = near_flags[0]
        for peer in range(1, inner):
            total = total + near_flags[peer]
        my_flag[1] = total
        far_flags[at_outer] = total

    def edge(side, device):
        return pltpu.make_async_remote_copy(
            src_ref=edge_out.at[side], dst_ref=edge_in.at[1 - side], send_sem=edge_send.at[side],
            recv_sem=edge_recv.at[1 - side], device_id=device, device_id_type=MESH)

    up, down = edge(0, {"sky": sky - 1}), edge(1, {"sky": sky + 1})

    def first_leg(side):
        return pltpu.make_async_remote_copy(
            src_ref=edge_out.at[side], dst_ref=detour, send_sem=edge_send.at[side], recv_sem=edge_recv.at[2],
            device_id={"chan": beside}, device_id_type=MESH)

    def second_leg(side):
        return pltpu.make_async_remote_copy(
            src_ref=detour, dst_ref=edge_in.at[1 - side], send_sem=edge_send.at[2],
            recv_sem=edge_recv.at[1 - side], device_id={"chan": served, "sky": beyond}, device_id_type=MESH)

    turns = ((0, jnp.logical_not(odd)), (1, odd))
    for side, turn in turns:
        there, copy = ((has_up, up), (has_down, down))[side]

        @pl.when(there & jnp.logical_not(detours & turn))
        def _():
            copy.start()

        @pl.when(detours & turn)
        def _():
            first_leg(side).start()

    if lean:
        each(1, lambda peer: tell(1, peer).start())

        @pl.loop(3, last)
        def _(step):
            reduce_for(chunks - 1 - step)
            send(step, False)

            @pl.when(step < last - 1)
            def _():
                reduce_for(step + 1)
                send(chunks - 1 - step, False)
    else:
        for step in range(2, AHEAD + 2):
            send_pair(step, True)
    keep(2, smooth(1, whole))
    if lean:
        send(last, False)
    keep(chunks - 1, smooth(chunks - 2, whole))

    keep(last + 1, jnp.zeros((size, width), F32))
    for spot in range(3):
        for half in range(2):
            tail_op[pl.ds((3 * half + spot) * size, size), :] = row_ops[
                last - 1 + spot, pl.ds(half * size, size), (2 - spot) * size:(3 - spot) * size]

    def tend(step):
        if not lean:
            @pl.when(step + AHEAD < last)
            def _():
                send_pair(step + AHEAD, True)

        for at in (step, chunks - 1 - step):
            keep(at + 1, smooth(at, whole))
        finish(step - 1)
        finish(chunks - step)

    @pl.loop(2, last - 3)
    def _(step):
        tend(step)

    for side, turn in turns:
        @pl.when(relays & turn)
        def _():
            first_leg(side).wait_recv()
            second_leg(side).start()

    @pl.loop(last - 3, last - 1)
    def _(step):
        tend(step)

    @pl.when(has_up)
    def _():
        down.wait_recv()
        keep(0, edge_in[0])

    @pl.when(has_down)
    def _():
        up.wait_recv()
        keep(chunks + 1, edge_in[1])

    @pl.when(jnp.logical_not(has_up))
    def _():
        keep(0, jnp.zeros((size, width), F32))

    @pl.when(jnp.logical_not(has_down))
    def _():
        keep(chunks + 1, jnp.zeros((size, width), F32))

    finish(0)
    finish(chunks - 1)
    keep(last, smooth(last - 1, whole))
    if lean:
        each(1, lambda peer: told(1, peer).wait_recv())
        total = far_flags[0]
        for peer in range(1, outer):
            total = total + far_flags[peer]
        flag[...] = total[:1, :1]

    ready = blend(1, own, last)
    for at in (last - 2, last + 1, last - 1, last):
        finish(at)

    arrive(last, whole)
    high, low = split(across(ready + blend(0, left_in, last, whole) + blend(2, right_in, last, whole)))
    three = 3 * size
    both = dot(tail_op[...], high)
    share = both[:three] + both[three:] + dot(tail_op[:three, :], low)
    for spot in range(3):
        out[last - 1 + spot] += share[spot * size:(spot + 1) * size]

    for side, turn in turns:
        @pl.when(relays & turn)
        def _():
            second_leg(side).wait_send()

    for (there, _), wait in zip(sides[2:], (up, down)):
        @pl.when(there)
        def _():
            wait.wait_send()

    if lean:
        for side in range(2):
            @pl.when(sides[side][0])
            def _():
                ask(side).wait_send()

        each(0, lambda peer: tell(0, peer).wait_send())
        each(1, lambda peer: tell(1, peer).wait_send())

    def sent(at, raw):
        @pl.when(has_right)
        def _():
            to_right(at, raw).wait_send()

        @pl.when(has_left)
        def _():
            to_left(at, raw).wait_send()

    sent(0, True)

    @pl.loop(1, chunks)
    def _(at):
        sent(at, whole)


def store(x):
    pieces = 4

    def body(x_ref, out_ref, sem):
        step = x.shape[0] // pieces
        copies = [pltpu.make_async_copy(x_ref.at[pl.ds(at * step, step)], out_ref.at[pl.ds(at * step, step)], sem.at[at])
                  for at in range(pieces)]
        for copy in copies:
            copy.start()
        for copy in copies:
            copy.wait()

    return pl.pallas_call(
        body, out_shape=pltpu.HBM(x.shape, x.dtype), in_specs=[pl.BlockSpec(memory_space=pltpu.VMEM)],
        out_specs=pl.BlockSpec(memory_space=pltpu.HBM), scratch_shapes=[pltpu.SemaphoreType.DMA((pieces,))],
        compiler_params=pltpu.CompilerParams(vmem_limit_bytes=1 << 20), name="store",
    )(pltpu.with_memory_space_constraint(x, pltpu.VMEM))


def solution(mesh):
    groups, skies = mesh.shape["chan"], mesh.shape["sky"]

    def regrid(lean, cube, shifts, halfwidth, taps, beam_rows, beam_cols):
        chunks, size, width = cube.shape
        height, chans = chunks * BAND, size // BAND
        thin = SLOTS * BAND
        inner = min(INNER, groups)
        outer = groups // inner
        whole = (chunks, size, width)
        vmem = pl.BlockSpec(memory_space=pltpu.VMEM)
        results, extra = [pltpu.VMEM(whole, F32)], []
        if lean:
            results.append(jax.ShapeDtypeStruct((1, 1), F32))
            extra = [
                pltpu.VMEM((2, chans, 128), F32),
                pltpu.VMEM((2, chans, 128), F32),
                pltpu.VMEM((chunks, 2 * thin, width), F32),
                pltpu.VMEM((4 * thin, 128), BF16),
                pltpu.VMEM((2, 2 * size, 128), BF16),
                pltpu.VMEM((inner, 8, 128), F32),
                pltpu.VMEM((outer, 8, 128), F32),
                pltpu.VMEM((2, 8, 128), F32),
                pltpu.SemaphoreType.DMA((2,)),
                pltpu.SemaphoreType.DMA((2,)),
                pltpu.SemaphoreType.DMA((2, max(inner, outer))),
                pltpu.SemaphoreType.DMA((2, max(inner, outer))),
            ]
        return pl.pallas_call(
            functools.partial(kernel, lean, groups, skies),
            out_shape=results,
            in_specs=[pl.BlockSpec(memory_space=pltpu.HBM)] * 6,
            out_specs=[vmem] * len(results),
            scratch_shapes=extra + [
                pltpu.SMEM(shifts.shape, jnp.int32),
                pltpu.SMEM(halfwidth.shape, jnp.int32),
                pltpu.VMEM(taps.shape, F32),
                pltpu.VMEM(whole, F32),
                pltpu.VMEM(whole, F32),
                pltpu.VMEM(whole, F32),
                pltpu.VMEM((chunks + 2, size, width), BF16),
                pltpu.VMEM((chunks + 2, size, width), BF16),
                pltpu.VMEM((6 * size, size), BF16),
                pltpu.VMEM((2, size, width), F32),
                pltpu.VMEM((2, size, width), F32),
                pltpu.VMEM((size, width), F32),
                pltpu.VMEM((width, width), F32),
                pltpu.VMEM((2, width, width), BF16),
                pltpu.VMEM((height, 3 * height), F32),
                pltpu.VMEM((chunks, 2 * size, 3 * size), BF16),
                pltpu.VMEM((2 * size, 3 * size), BF16),
                pltpu.SemaphoreType.DMA((8,)),
                pltpu.SemaphoreType.DMA((2, chunks)),
                pltpu.SemaphoreType.DMA((2, chunks)),
                pltpu.SemaphoreType.DMA((3,)),
                pltpu.SemaphoreType.DMA((3,)),
            ],
            compiler_params=pltpu.CompilerParams(
                collective_id=int(lean), has_side_effects=True, vmem_limit_bytes=40 << 20),
            name="regrid" if lean else "regrid_whole",
        )(*(pltpu.with_memory_space_constraint(x, pltpu.HBM) for x in (
            cube, shifts, halfwidth, taps, beam_rows, beam_cols)))

    def per_device(cube, *others):
        height, chans, width = cube.shape
        args = (cube.reshape(height // BAND, BAND * chans, width), *others)
        result, flag = regrid(True, *args)
        result, _ = lax.while_loop(
            lambda state: state[1] > 0.5,
            lambda state: (store(regrid(False, *args)[0]), jnp.zeros((), F32)),
            (store(result), flag[0, 0]))
        return result.reshape(cube.shape)

    return jax.shard_map(
        per_device,
        mesh=mesh,
        in_specs=(P("sky", "chan", None), P("chan"), P("chan"), P("chan", None), P(), P()),
        out_specs=P("sky", "chan", None),
        check_vma=False,
    )
```

```python
import functools

import jax
import jax.numpy as jnp
from jax import lax
from jax.experimental import pallas as pl
from jax.experimental.pallas import tpu as pltpu
from jax.sharding import PartitionSpec as P

BLK = 4
S_MAX = 12
RADIUS = 4
BAND = 8
SLOTS = 12
AHEAD = 2
RUN = 4
INNER = 8
MESH = pl.DeviceIdType.MESH
BF16 = jnp.bfloat16
F32 = jnp.float32
ACROSS = (((1,), (1,)), ((), ()))


def split(x):
    high = x.astype(BF16)
    return high, (x - high.astype(F32)).astype(BF16)


def dot(a, b):
    return jnp.dot(a, b, preferred_element_type=F32)


def dot_across(a, b):
    return lax.dot_general(a, b, ACROSS, preferred_element_type=F32)


def iota(shape, dim):
    return lax.broadcasted_iota(jnp.int32, shape, dim)


def ones_where(condition):
    return jnp.where(condition, 1.0, 0.0).astype(BF16)


def deepen(x):
    return jnp.concatenate([x, jnp.zeros((128 - x.shape[0], x.shape[1]), x.dtype)], axis=0)


def need(band):
    shape = band.shape
    row, lane = iota(shape, 0), iota(shape, 1)
    ones, before = jnp.ones((128, 128), BF16), ones_where(iota((128, 128), 0) < iota((128, 128), 1))
    one_rows = ones[:shape[0]]
    pattern = ones_where(band != 0.0)
    high, low = split(band)
    raw = jnp.zeros(shape, F32)
    for block in range(shape[0] // BLK):
        raw = jnp.where(lane // BLK == block, (row // 2 ** block % 2).astype(F32), raw)
    touched = jnp.where(dot_across(one_rows, deepen(pattern)) > 0.5, 1.0, 0.0)
    channels = ones_where(dot(raw.astype(BF16), deepen(pattern)) > 0.5)
    cost = dot(channels, ones) + dot((touched * (1.0 - raw)).astype(BF16), ones)
    score = cost * shape[0] + row.astype(F32)
    best = jnp.min(score, axis=0, keepdims=True)
    chosen = jnp.sum(jnp.where(score == best, raw, 0.0), axis=0, keepdims=True)
    raw = dot(ones_where((row == lane) & (chosen > 0.5)), ones)
    pattern_raw = (pattern.astype(F32) * raw).astype(BF16)
    pattern_out = (pattern.astype(F32) * (1.0 - raw)).astype(BF16)
    hit = ones_where(dot(one_rows, deepen(pattern_raw)) > 0.5)
    channels = dot(hit, ones)
    pick_raw = ones_where((dot(hit, before) == row.astype(F32)) & (hit > 0.5))
    hit = ones_where(dot_across(one_rows, deepen(pattern_out)) > 0.5)
    count = channels + dot(hit, ones)
    pick_out = ones_where((channels + dot(hit, before) == row.astype(F32)) & (hit > 0.5))
    send = pick_raw.astype(F32) + (dot(pick_out, deepen(high)) + dot(pick_out, deepen(low)))
    hit = ones_where(dot(pattern_out, ones) > 0.5)
    place = channels + dot(ones_where(lane < row), deepen(hit))
    receive_out = jnp.where((place == lane.astype(F32)) & (hit > 0.5), 1.0, 0.0)
    high_raw = dot_across((high.astype(F32) * raw).astype(BF16), deepen(pick_raw))
    low_raw = dot_across((low.astype(F32) * raw).astype(BF16), deepen(pick_raw))
    return send, ((receive_out + high_raw).astype(BF16), low_raw.astype(BF16)), count


def kernel(lean, groups, skies, *refs):
    cube, shifts_in, halfwidth_in, taps_in, beam_rows, beam_cols, out, *refs = refs
    if lean:
        flag, needs, asked, for_both, send_op, receive_ops, my_flag, ring, flag_in, *refs = refs
        need_send, need_recv, ring_send, ring_recv, flag_send, flag_recv, *refs = refs
    (shifts, halfwidth, taps, own, left_in, right_in, spread, spread_low, tail_op, edge_out, edge_in, detour, cols,
     cols_pair, rows, row_ops, chan_op, local_sem, send_sem, recv_sem, edge_send, edge_recv) = refs
    chunks, size, width = cube.shape
    chans = size // BAND
    reach = S_MAX + RADIUS
    thin = SLOTS * BAND
    last = chunks // 2
    group, sky = lax.axis_index("chan"), lax.axis_index("sky")
    has_left, has_right = group > 0, group < groups - 1
    has_up, has_down = sky > 0, sky < skies - 1
    inner = min(INNER, groups)
    outer = groups // inner
    spot = lax.rem(group, RUN)
    odd = lax.rem(sky, 2) == 1
    crosses = jnp.where(odd, has_down, has_up)
    beyond = jnp.where(odd, sky + 1, sky - 1)
    beside = jnp.where(spot == 0, group + 1, group - 1)
    detours = crosses & ((spot == 0) | (spot == RUN - 1)) & (beside < groups)
    served = jnp.where(spot == 1, group - 1, group + 1)
    relays = crosses & ((spot == 1) | (spot == RUN - 2)) & (served < groups)

    barrier = pltpu.get_barrier_semaphore()
    sides = [(has_left, {"chan": group - 1}), (has_right, {"chan": group + 1}),
             (has_up, {"sky": sky - 1}), (has_down, {"sky": sky + 1})]
    waits = relays.astype(jnp.int32)
    for there, device in sides:
        @pl.when(there)
        def _():
            pl.semaphore_signal(barrier, inc=1, device_id=device, device_id_type=MESH)

        waits = waits + there.astype(jnp.int32)
    middle = (spot == 1) | (spot == RUN - 2)
    start = group - lax.rem(group, inner)
    hops = (outer // 2, (outer - 1) // 2)
    around = [{"chan": lax.rem(group + inner, groups)}, {"chan": lax.rem(group + groups - inner, groups)}]
    facing = {"chan": start + lax.rem(group - start + RUN, inner)}
    partners = (around if outer > 1 else []) + ([facing] if inner > RUN else [])
    if lean and partners:
        @pl.when(middle)
        def _():
            for device in partners:
                pl.semaphore_signal(barrier, inc=1, device_id=device, device_id_type=MESH)

        waits = waits + len(partners) * middle.astype(jnp.int32)

    @pl.when(detours)
    def _():
        pl.semaphore_signal(barrier, inc=1, device_id={"chan": beside, "sky": beyond}, device_id_type=MESH)

    height = chunks * BAND
    local = [
        pltpu.make_async_copy(shifts_in, shifts, local_sem.at[5]),
        pltpu.make_async_copy(halfwidth_in, halfwidth, local_sem.at[6]),
        pltpu.make_async_copy(taps_in, taps, local_sem.at[7]),
        pltpu.make_async_copy(cube, own, local_sem.at[0]),
        pltpu.make_async_copy(beam_cols, cols, local_sem.at[1]),
    ]
    for part in range(3):
        block = lax.rem(sky + skies + part - 1, skies)
        local.append(pltpu.make_async_copy(
            beam_rows.at[pl.ds(pl.multiple_of(sky * height, height), height),
                         pl.ds(pl.multiple_of(block * height, height), height)],
            rows.at[:, pl.ds(part * height, height)], local_sem.at[2 + part]))
    for copy in local:
        copy.start()
    for copy in local[:3]:
        copy.wait()

    chan = iota((chans, 128), 0)
    place = iota((chans, 128), 1)
    offsets = jnp.zeros((chans, 128), jnp.int32)
    limits = jnp.zeros((chans, 2 * RADIUS + 1), jnp.int32)
    for block in range(chans // BLK):
        offsets = jnp.where(chan // BLK == block, shifts[block], offsets)
        limits = jnp.where(iota(limits.shape, 0) // BLK == block, halfwidth[block], limits)
    masked = jnp.where(jnp.abs(iota(limits.shape, 1) - RADIUS) <= limits, taps[...], 0.0)
    weights = masked / jnp.sum(masked, axis=1, keepdims=True)

    def slab(base):
        band = jnp.zeros((chans, 128), F32)
        for tap in range(2 * RADIUS + 1):
            spot = chan + reach + offsets + (tap - RADIUS) - base
            band = band + jnp.where((place == spot) & (place < chans), weights[:, tap:tap + 1], 0.0)
        return band

    left_band = jnp.where(has_left, slab(0), 0.0)
    right_band = jnp.where(has_right, slab(2 * chans), 0.0)
    bands = (left_band, slab(chans), right_band)

    if lean:
        receives = []
        over = jnp.zeros((chans, 128), F32)
        for side, band in enumerate((bands[0], bands[2])):
            send, receive, count = need(band)
            receives.append((send, receive))
            over = over + jnp.where(count > SLOTS + 0.5, 1.0, 0.0)
        for side in range(2):
            needs[side] = jnp.where(place < 64, receives[side][0], over)

        @pl.when(jnp.logical_not(has_left))
        def _():
            asked[0] = jnp.zeros((chans, 128), F32)

        @pl.when(jnp.logical_not(has_right))
        def _():
            asked[1] = jnp.zeros((chans, 128), F32)

    pl.semaphore_wait(barrier, waits)

    def thinned(ref, at, raw):
        return ref.at[at] if raw else ref.at[at, pl.ds(0, thin)]

    def to_right(at, raw):
        return pltpu.make_async_remote_copy(
            src_ref=cube.at[at] if raw else for_both.at[at, pl.ds(thin, thin)], dst_ref=thinned(left_in, at, raw),
            send_sem=send_sem.at[0, at], recv_sem=recv_sem.at[0, at],
            device_id={"chan": group + 1}, device_id_type=MESH)

    def to_left(at, raw):
        return pltpu.make_async_remote_copy(
            src_ref=cube.at[at] if raw else for_both.at[at, pl.ds(0, thin)], dst_ref=thinned(right_in, at, raw),
            send_sem=send_sem.at[1, at], recv_sem=recv_sem.at[1, at],
            device_id={"chan": group - 1}, device_id_type=MESH)

    def send(at, raw):
        @pl.when(has_right)
        def _():
            to_right(at, raw).start()

        @pl.when(has_left)
        def _():
            to_left(at, raw).start()

    def send_pair(step, raw):
        send(step, raw)
        send(chunks - 1 - step, raw)

    def ask(side):
        return pltpu.make_async_remote_copy(
            src_ref=needs.at[side], dst_ref=asked.at[1 - side], send_sem=need_send.at[side],
            recv_sem=need_recv.at[1 - side], device_id=sides[side][1], device_id_type=MESH)

    def pass_on(way, hop):
        return pltpu.make_async_remote_copy(
            src_ref=my_flag.at[0] if hop == 0 else ring.at[way, hop - 1], dst_ref=ring.at[way, hop],
            send_sem=ring_send.at[way, hop], recv_sem=ring_recv.at[way, hop], device_id=around[way],
            device_id_type=MESH)

    def turn_ring(hop):
        if not lean or outer == 1 or hop > max(hops):
            return

        @pl.when(middle)
        def _():
            for way in range(2):
                if 0 < hop <= hops[way]:
                    pass_on(way, hop - 1).wait_recv()
                if hop < hops[way]:
                    pass_on(way, hop).start()

    inward = jnp.where(spot == 1, group + 1, group - 1)
    outward = jnp.where(spot == 1, group - 1, group + 1)

    def tell(stage, device):
        return pltpu.make_async_remote_copy(
            src_ref=my_flag.at[1 + stage], dst_ref=flag_in.at[stage], send_sem=flag_send.at[stage],
            recv_sem=flag_recv.at[stage], device_id=device, device_id_type=MESH)

    tells = (tell(0, facing), tell(1, {"chan": inward}), tell(2, {"chan": outward})) if lean else ()

    if lean:
        for side in range(2):
            @pl.when(sides[side][0])
            def _():
                ask(side).start()

    send(0, True)
    if not lean:
        send(chunks - 1, True)
        send_pair(1, True)

    @pl.when(jnp.logical_not(has_left))
    def _():
        left_in[...] = jnp.zeros(left_in.shape, F32)

    @pl.when(jnp.logical_not(has_right))
    def _():
        right_in[...] = jnp.zeros(right_in.shape, F32)

    for copy in local[3:]:
        copy.wait()

    def apply(op, value, rows_out):
        high, low = split(value)
        both = dot(op, high)
        return both[:rows_out] + both[rows_out:] + dot(op[:rows_out], low)

    def reduce_for(at):
        for_both[at] = apply(send_op[...], own[at], 2 * thin)

    pick = ones_where(iota((128, size), 0) == iota((128, size), 1) % chans)
    same_row = iota((size, size), 0) // chans == iota((size, size), 1) // chans
    for slot, band in enumerate(bands):
        for half, part in enumerate(split(band)):
            wide = jnp.concatenate([dot(part, pick)] * BAND, axis=0)
            chan_op[pl.ds(half * size, size), pl.ds(slot * size, size)] = jnp.where(same_row, wide, 0.0).astype(BF16)
    if lean:
        pick = ones_where(iota((128, 128), 0) == iota((128, 128), 1) // BAND)
        same_row = iota((size, 128), 0) // chans == iota((size, 128), 1) % BAND
        for side, (_, receive) in enumerate(receives):
            for half, part in enumerate(receive):
                wide = jnp.concatenate([dot(part, pick)] * BAND, axis=0)
                receive_ops[side, pl.ds(half * size, size), :] = jnp.where(same_row, wide, 0.0).astype(BF16)

        for side in range(2):
            @pl.when(sides[side][0])
            def _():
                ask(1 - side).wait_recv()

        my_flag[0] = needs[0, :8] + asked[0, :8] + asked[1, :8]
        pick = ones_where(iota((128, 128), 0) == iota((128, 128), 1) % chans)
        same_row = iota((128, 128), 0) % BAND == iota((128, 128), 1) // chans
        for side in range(2):
            for half, part in enumerate(split(asked[side])):
                wide = jnp.broadcast_to(dot(part, pick)[:, None, :], (chans, BAND, 128)).reshape(128, 128)
                send_op[pl.ds((2 * half + side) * thin, thin), :] = jnp.where(same_row, wide, 0.0)[:thin].astype(BF16)
        reduce_for(chunks - 1)
        reduce_for(1)
        send(chunks - 1, False)
        turn_ring(0)
        reduce_for(chunks - 2)
        send(1, False)

    high, low = split(cols[...])
    cols_pair[0] = high
    cols_pair[1] = low
    turn_ring(1)

    pick = ones_where(iota((128, 3 * size), 0) == iota((128, 3 * size), 1) // chans)
    same_chan = iota((size, 3 * size), 0) % chans == iota((size, 3 * size), 1) % chans
    for at in range(chunks):
        start = height + (at - 1) * BAND
        close = rows[pl.ds(at * BAND, BAND), start:start + 3 * BAND]
        close = jnp.concatenate([close, jnp.zeros((BAND, 128 - 3 * BAND), F32)], axis=1)
        for half, part in enumerate(split(close)):
            wide = dot(part, pick)
            wide = jnp.broadcast_to(wide[:, None, :], (BAND, chans, 3 * size)).reshape(size, 3 * size)
            row_ops[at, pl.ds(half * size, size), :] = jnp.where(same_chan, wide, 0.0).astype(BF16)

    if lean:
        turn_ring(2)
        reduce_for(2)
        send(chunks - 2, False)

    def keep(at, value):
        high, low = split(value)
        spread[at] = high
        spread_low[at] = low

    def arrive(at, raw):
        @pl.when(has_left)
        def _():
            to_right(at, raw).wait_recv()

        @pl.when(has_right)
        def _():
            to_left(at, raw).wait_recv()

    def blend(part, ref, at, raw=True):
        if raw:
            return apply(chan_op[:, part * size:(part + 1) * size], ref[at], size)
        return apply(receive_ops[part // 2, :, :thin], ref[at, pl.ds(0, thin)], size)

    def across(total):
        high, low = split(total)
        both = dot_across(jnp.concatenate([high, low], axis=0), cols_pair[0])
        return both[:size] + both[size:] + dot_across(high, cols_pair[1])

    def smooth(at, raw):
        arrive(at, raw)
        return across(blend(1, own, at) + blend(0, left_in, at, raw) + blend(2, right_in, at, raw))

    def finish(at):
        op = row_ops[at]
        both = dot(op, spread[pl.ds(at, 3)].reshape(3 * size, width))
        out[at] = both[:size] + both[size:] + dot(op[:size], spread_low[pl.ds(at, 3)].reshape(3 * size, width))

    whole = not lean
    for side, at in enumerate((0, chunks - 1)):
        value = smooth(at, at == 0 or whole)
        edge_out[side] = value
        keep(at + 1, value)
        if lean:
            turn_ring(3 + side)
            reduce_for((chunks - 3, 3)[side])
            send((2, chunks - 3)[side], False)
    if lean:
        for hop in range(5, max(hops) + 1):
            turn_ring(hop)

        @pl.when(middle)
        def _():
            total = my_flag[0]
            for way in range(2):
                for hop in range(hops[way]):
                    total = total + ring[way, hop]
            my_flag[1] = total

    def edge(side, device):
        return pltpu.make_async_remote_copy(
            src_ref=edge_out.at[side], dst_ref=edge_in.at[1 - side], send_sem=edge_send.at[side],
            recv_sem=edge_recv.at[1 - side], device_id=device, device_id_type=MESH)

    up, down = edge(0, {"sky": sky - 1}), edge(1, {"sky": sky + 1})

    def first_leg(side):
        return pltpu.make_async_remote_copy(
            src_ref=edge_out.at[side], dst_ref=detour, send_sem=edge_send.at[side], recv_sem=edge_recv.at[2],
            device_id={"chan": beside}, device_id_type=MESH)

    def second_leg(side):
        return pltpu.make_async_remote_copy(
            src_ref=detour, dst_ref=edge_in.at[1 - side], send_sem=edge_send.at[2],
            recv_sem=edge_recv.at[1 - side], device_id={"chan": served, "sky": beyond}, device_id_type=MESH)

    turns = ((0, jnp.logical_not(odd)), (1, odd))
    for side, turn in turns:
        there, copy = ((has_up, up), (has_down, down))[side]

        @pl.when(there & jnp.logical_not(detours & turn))
        def _():
            copy.start()

        @pl.when(detours & turn)
        def _():
            first_leg(side).start()

    if lean:
        reduce_for(chunks - 4)
        send(3, False)
        if inner > RUN:
            @pl.when(middle)
            def _():
                tells[0].start()

        reduce_for(4)
        send(chunks - 4, False)
    else:
        for step in range(2, AHEAD + 2):
            send_pair(step, True)
    keep(2, smooth(1, whole))
    if lean:
        @pl.when(middle)
        def _():
            total = my_flag[1]
            if inner > RUN:
                tells[0].wait_recv()
                total = total + flag_in[0]
            my_flag[2] = total

    keep(chunks - 1, smooth(chunks - 2, whole))
    if lean:
        @pl.when(middle)
        def _():
            tells[1].start()

        @pl.loop(4, last)
        def _(step):
            reduce_for(chunks - 1 - step)
            send(step, False)

            @pl.when(step < last - 1)
            def _():
                reduce_for(step + 1)
                send(chunks - 1 - step, False)

    keep(last + 1, jnp.zeros((size, width), F32))
    for spot in range(3):
        for half in range(2):
            tail_op[pl.ds((3 * half + spot) * size, size), :] = row_ops[
                last - 1 + spot, pl.ds(half * size, size), (2 - spot) * size:(3 - spot) * size]

    def tend(step):
        if not lean:
            @pl.when(step + AHEAD < last)
            def _():
                send_pair(step + AHEAD, True)

        for at in (step, chunks - 1 - step):
            keep(at + 1, smooth(at, whole))
        finish(step - 1)
        finish(chunks - step)

    tend(2)
    if lean:
        send(last, False)

    @pl.loop(3, last - 3)
    def _(step):
        tend(step)

    if lean:
        @pl.when(middle)
        def _():
            tells[1].wait_recv()
            my_flag[3] = my_flag[2] + flag_in[1]

    for side, turn in turns:
        @pl.when(relays & turn)
        def _():
            first_leg(side).wait_recv()
            second_leg(side).start()

    @pl.loop(last - 3, last - 1)
    def _(step):
        tend(step)

    @pl.when(has_up)
    def _():
        down.wait_recv()
        keep(0, edge_in[0])

    @pl.when(has_down)
    def _():
        up.wait_recv()
        keep(chunks + 1, edge_in[1])

    @pl.when(jnp.logical_not(has_up))
    def _():
        keep(0, jnp.zeros((size, width), F32))

    @pl.when(jnp.logical_not(has_down))
    def _():
        keep(chunks + 1, jnp.zeros((size, width), F32))

    finish(0)
    finish(chunks - 1)
    keep(last, smooth(last - 1, whole))
    if lean:
        @pl.when(middle)
        def _():
            tells[2].start()
            flag[...] = my_flag[3, :1, 64:65]

    ready = blend(1, own, last)
    for at in (last - 2, last + 1, last - 1, last):
        finish(at)

    arrive(last, whole)
    high, low = split(across(ready + blend(0, left_in, last, whole) + blend(2, right_in, last, whole)))
    three = 3 * size
    both = dot(tail_op[...], high)
    share = both[:three] + both[three:] + dot(tail_op[:three, :], low)
    for spot in range(3):
        out[last - 1 + spot] += share[spot * size:(spot + 1) * size]

    if lean:
        @pl.when(jnp.logical_not(middle))
        def _():
            tells[2].wait_recv()
            flag[...] = flag_in[2, :1, 64:65]

        @pl.when(middle)
        def _():
            for copy in tells[inner == RUN:]:
                copy.wait_send()
            if outer > 1:
                for way in range(2):
                    for hop in range(hops[way]):
                        pass_on(way, hop).wait_send()

    for side, turn in turns:
        @pl.when(relays & turn)
        def _():
            second_leg(side).wait_send()

    for (there, _), wait in zip(sides[2:], (up, down)):
        @pl.when(there)
        def _():
            wait.wait_send()

    if lean:
        for side in range(2):
            @pl.when(sides[side][0])
            def _():
                ask(side).wait_send()

    def sent(at, raw):
        @pl.when(has_right)
        def _():
            to_right(at, raw).wait_send()

        @pl.when(has_left)
        def _():
            to_left(at, raw).wait_send()

    sent(0, True)

    @pl.loop(1, chunks)
    def _(at):
        sent(at, whole)


def store(x):
    pieces = 4

    def body(x_ref, out_ref, sem):
        step = x.shape[0] // pieces
        copies = [pltpu.make_async_copy(x_ref.at[pl.ds(at * step, step)], out_ref.at[pl.ds(at * step, step)], sem.at[at])
                  for at in range(pieces)]
        for copy in copies:
            copy.start()
        for copy in copies:
            copy.wait()

    return pl.pallas_call(
        body, out_shape=pltpu.HBM(x.shape, x.dtype), in_specs=[pl.BlockSpec(memory_space=pltpu.VMEM)],
        out_specs=pl.BlockSpec(memory_space=pltpu.HBM), scratch_shapes=[pltpu.SemaphoreType.DMA((pieces,))],
        compiler_params=pltpu.CompilerParams(vmem_limit_bytes=1 << 20), name="store",
    )(pltpu.with_memory_space_constraint(x, pltpu.VMEM))


def solution(mesh):
    groups, skies = mesh.shape["chan"], mesh.shape["sky"]

    def regrid(lean, cube, shifts, halfwidth, taps, beam_rows, beam_cols):
        chunks, size, width = cube.shape
        height, chans = chunks * BAND, size // BAND
        thin = SLOTS * BAND
        inner = min(INNER, groups)
        outer = groups // inner
        whole = (chunks, size, width)
        vmem = pl.BlockSpec(memory_space=pltpu.VMEM)
        results, extra = [pltpu.VMEM(whole, F32)], []
        if lean:
            results.append(jax.ShapeDtypeStruct((1, 1), F32))
            extra = [
                pltpu.VMEM((2, chans, 128), F32),
                pltpu.VMEM((2, chans, 128), F32),
                pltpu.VMEM((chunks, 2 * thin, width), F32),
                pltpu.VMEM((4 * thin, 128), BF16),
                pltpu.VMEM((2, 2 * size, 128), BF16),
                pltpu.VMEM((4, 8, 128), F32),
                pltpu.VMEM((2, max(outer // 2, 1), 8, 128), F32),
                pltpu.VMEM((3, 8, 128), F32),
                pltpu.SemaphoreType.DMA((2,)),
                pltpu.SemaphoreType.DMA((2,)),
                pltpu.SemaphoreType.DMA((2, max(outer // 2, 1))),
                pltpu.SemaphoreType.DMA((2, max(outer // 2, 1))),
                pltpu.SemaphoreType.DMA((3,)),
                pltpu.SemaphoreType.DMA((3,)),
            ]
        return pl.pallas_call(
            functools.partial(kernel, lean, groups, skies),
            out_shape=results,
            in_specs=[pl.BlockSpec(memory_space=pltpu.HBM)] * 6,
            out_specs=[vmem] * len(results),
            scratch_shapes=extra + [
                pltpu.SMEM(shifts.shape, jnp.int32),
                pltpu.SMEM(halfwidth.shape, jnp.int32),
                pltpu.VMEM(taps.shape, F32),
                pltpu.VMEM(whole, F32),
                pltpu.VMEM(whole, F32),
                pltpu.VMEM(whole, F32),
                pltpu.VMEM((chunks + 2, size, width), BF16),
                pltpu.VMEM((chunks + 2, size, width), BF16),
                pltpu.VMEM((6 * size, size), BF16),
                pltpu.VMEM((2, size, width), F32),
                pltpu.VMEM((2, size, width), F32),
                pltpu.VMEM((size, width), F32),
                pltpu.VMEM((width, width), F32),
                pltpu.VMEM((2, width, width), BF16),
                pltpu.VMEM((height, 3 * height), F32),
                pltpu.VMEM((chunks, 2 * size, 3 * size), BF16),
                pltpu.VMEM((2 * size, 3 * size), BF16),
                pltpu.SemaphoreType.DMA((8,)),
                pltpu.SemaphoreType.DMA((2, chunks)),
                pltpu.SemaphoreType.DMA((2, chunks)),
                pltpu.SemaphoreType.DMA((3,)),
                pltpu.SemaphoreType.DMA((3,)),
            ],
            compiler_params=pltpu.CompilerParams(
                collective_id=int(lean), has_side_effects=True, vmem_limit_bytes=40 << 20),
            name="regrid" if lean else "regrid_whole",
        )(*(pltpu.with_memory_space_constraint(x, pltpu.HBM) for x in (
            cube, shifts, halfwidth, taps, beam_rows, beam_cols)))

    def per_device(cube, *others):
        height, chans, width = cube.shape
        args = (cube.reshape(height // BAND, BAND * chans, width), *others)
        result, flag = regrid(True, *args)
        result, _ = lax.while_loop(
            lambda state: state[1] > 0.5,
            lambda state: (store(regrid(False, *args)[0]), jnp.zeros((), F32)),
            (store(result), flag[0, 0]))
        return result.reshape(cube.shape)

    return jax.shard_map(
        per_device,
        mesh=mesh,
        in_specs=(P("sky", "chan", None), P("chan"), P("chan"), P("chan", None), P(), P()),
        out_specs=P("sky", "chan", None),
        check_vma=False,
    )
```

```python
import functools

import jax
import jax.numpy as jnp
from jax import lax
from jax.experimental import pallas as pl
from jax.experimental.pallas import tpu as pltpu
from jax.sharding import PartitionSpec as P

BLK = 4
S_MAX = 12
RADIUS = 4
BAND = 8
SLOTS = 12
AHEAD = 2
RUN = 4
INNER = 8
MESH = pl.DeviceIdType.MESH
BF16 = jnp.bfloat16
F32 = jnp.float32
ACROSS = (((1,), (1,)), ((), ()))


def split(x):
    high = x.astype(BF16)
    return high, (x - high.astype(F32)).astype(BF16)


def dot(a, b):
    return jnp.dot(a, b, preferred_element_type=F32)


def dot_across(a, b):
    return lax.dot_general(a, b, ACROSS, preferred_element_type=F32)


def iota(shape, dim):
    return lax.broadcasted_iota(jnp.int32, shape, dim)


def ones_where(condition):
    return jnp.where(condition, 1.0, 0.0).astype(BF16)


def deepen(x):
    return jnp.concatenate([x, jnp.zeros((128 - x.shape[0], x.shape[1]), x.dtype)], axis=0)


def need(band):
    shape = band.shape
    row, lane = iota(shape, 0), iota(shape, 1)
    ones, before = jnp.ones((128, 128), BF16), ones_where(iota((128, 128), 0) < iota((128, 128), 1))
    one_rows = ones[:shape[0]]
    pattern = ones_where(band != 0.0)
    high, low = split(band)
    raw = jnp.zeros(shape, F32)
    for block in range(shape[0] // BLK):
        raw = jnp.where(lane // BLK == block, (row // 2 ** block % 2).astype(F32), raw)
    touched = jnp.where(dot_across(one_rows, deepen(pattern)) > 0.5, 1.0, 0.0)
    channels = ones_where(dot(raw.astype(BF16), deepen(pattern)) > 0.5)
    cost = dot(channels, ones) + dot((touched * (1.0 - raw)).astype(BF16), ones)
    score = cost * shape[0] + row.astype(F32)
    best = jnp.min(score, axis=0, keepdims=True)
    chosen = jnp.sum(jnp.where(score == best, raw, 0.0), axis=0, keepdims=True)
    raw = dot(ones_where((row == lane) & (chosen > 0.5)), ones)
    pattern_raw = (pattern.astype(F32) * raw).astype(BF16)
    pattern_out = (pattern.astype(F32) * (1.0 - raw)).astype(BF16)
    hit = ones_where(dot(one_rows, deepen(pattern_raw)) > 0.5)
    channels = dot(hit, ones)
    pick_raw = ones_where((dot(hit, before) == row.astype(F32)) & (hit > 0.5))
    hit = ones_where(dot_across(one_rows, deepen(pattern_out)) > 0.5)
    count = channels + dot(hit, ones)
    pick_out = ones_where((channels + dot(hit, before) == row.astype(F32)) & (hit > 0.5))
    send = pick_raw.astype(F32) + (dot(pick_out, deepen(high)) + dot(pick_out, deepen(low)))
    hit = ones_where(dot(pattern_out, ones) > 0.5)
    place = channels + dot(ones_where(lane < row), deepen(hit))
    receive_out = jnp.where((place == lane.astype(F32)) & (hit > 0.5), 1.0, 0.0)
    high_raw = dot_across((high.astype(F32) * raw).astype(BF16), deepen(pick_raw))
    low_raw = dot_across((low.astype(F32) * raw).astype(BF16), deepen(pick_raw))
    return send, ((receive_out + high_raw).astype(BF16), low_raw.astype(BF16)), count


def kernel(lean, groups, skies, *refs):
    cube, shifts_in, halfwidth_in, taps_in, beam_rows, beam_cols, out, *refs = refs
    if lean:
        flag, needs, asked, for_both, send_op, receive_ops, my_flag, ring, flag_in, *refs = refs
        need_send, need_recv, ring_send, ring_recv, flag_send, flag_recv, *refs = refs
    (shifts, halfwidth, taps, own, left_in, right_in, spread, spread_low, tail_op, edge_out, edge_in, detour, cols,
     cols_pair, rows, row_ops, chan_op, local_sem, send_sem, recv_sem, edge_send, edge_recv) = refs
    chunks, size, width = cube.shape
    chans = size // BAND
    reach = S_MAX + RADIUS
    thin = SLOTS * BAND
    last = chunks // 2
    group, sky = lax.axis_index("chan"), lax.axis_index("sky")
    has_left, has_right = group > 0, group < groups - 1
    has_up, has_down = sky > 0, sky < skies - 1
    inner = min(INNER, groups)
    outer = groups // inner
    spot = lax.rem(group, RUN)
    odd = lax.rem(sky, 2) == 1
    crosses = jnp.where(odd, has_down, has_up)
    beyond = jnp.where(odd, sky + 1, sky - 1)
    beside = jnp.where(spot == 0, group + 1, group - 1)
    detours = crosses & ((spot == 0) | (spot == RUN - 1)) & (beside < groups)
    served = jnp.where(spot == 1, group - 1, group + 1)
    relays = crosses & ((spot == 1) | (spot == RUN - 2)) & (served < groups)

    barrier = pltpu.get_barrier_semaphore()
    sides = [(has_left, {"chan": group - 1}), (has_right, {"chan": group + 1}),
             (has_up, {"sky": sky - 1}), (has_down, {"sky": sky + 1})]
    waits = relays.astype(jnp.int32)
    for there, device in sides:
        @pl.when(there)
        def _():
            pl.semaphore_signal(barrier, inc=1, device_id=device, device_id_type=MESH)

        waits = waits + there.astype(jnp.int32)
    middle = (spot == 1) | (spot == RUN - 2)
    start = group - lax.rem(group, inner)
    hops = (outer // 2, (outer - 1) // 2)
    around = [{"chan": lax.rem(group + inner, groups)}, {"chan": lax.rem(group + groups - inner, groups)}]
    facing = {"chan": start + lax.rem(group - start + RUN, inner)}
    partners = (around if outer > 1 else []) + ([facing] if inner > RUN else [])
    if lean and partners:
        @pl.when(middle)
        def _():
            for device in partners:
                pl.semaphore_signal(barrier, inc=1, device_id=device, device_id_type=MESH)

        waits = waits + len(partners) * middle.astype(jnp.int32)

    @pl.when(detours)
    def _():
        pl.semaphore_signal(barrier, inc=1, device_id={"chan": beside, "sky": beyond}, device_id_type=MESH)

    height = chunks * BAND
    local = [
        pltpu.make_async_copy(shifts_in, shifts, local_sem.at[5]),
        pltpu.make_async_copy(halfwidth_in, halfwidth, local_sem.at[6]),
        pltpu.make_async_copy(taps_in, taps, local_sem.at[7]),
        pltpu.make_async_copy(cube, own, local_sem.at[0]),
        pltpu.make_async_copy(beam_cols, cols, local_sem.at[1]),
    ]
    for part in range(3):
        block = lax.rem(sky + skies + part - 1, skies)
        local.append(pltpu.make_async_copy(
            beam_rows.at[pl.ds(pl.multiple_of(sky * height, height), height),
                         pl.ds(pl.multiple_of(block * height, height), height)],
            rows.at[:, pl.ds(part * height, height)], local_sem.at[2 + part]))
    for copy in local:
        copy.start()
    for copy in local[:3]:
        copy.wait()

    chan = iota((chans, 128), 0)
    place = iota((chans, 128), 1)
    offsets = jnp.zeros((chans, 128), jnp.int32)
    limits = jnp.zeros((chans, 2 * RADIUS + 1), jnp.int32)
    for block in range(chans // BLK):
        offsets = jnp.where(chan // BLK == block, shifts[block], offsets)
        limits = jnp.where(iota(limits.shape, 0) // BLK == block, halfwidth[block], limits)
    masked = jnp.where(jnp.abs(iota(limits.shape, 1) - RADIUS) <= limits, taps[...], 0.0)
    weights = masked / jnp.sum(masked, axis=1, keepdims=True)

    def slab(base):
        band = jnp.zeros((chans, 128), F32)
        for tap in range(2 * RADIUS + 1):
            spot = chan + reach + offsets + (tap - RADIUS) - base
            band = band + jnp.where((place == spot) & (place < chans), weights[:, tap:tap + 1], 0.0)
        return band

    left_band = jnp.where(has_left, slab(0), 0.0)
    right_band = jnp.where(has_right, slab(2 * chans), 0.0)
    bands = (left_band, slab(chans), right_band)

    if lean:
        receives = []
        over = jnp.zeros((chans, 128), F32)
        for side, band in enumerate((bands[0], bands[2])):
            send, receive, count = need(band)
            receives.append((send, receive))
            over = over + jnp.where(count > SLOTS + 0.5, 1.0, 0.0)
        for side in range(2):
            needs[side] = jnp.where(place < 64, receives[side][0], over)

        @pl.when(jnp.logical_not(has_left))
        def _():
            asked[0] = jnp.zeros((chans, 128), F32)

        @pl.when(jnp.logical_not(has_right))
        def _():
            asked[1] = jnp.zeros((chans, 128), F32)

    pl.semaphore_wait(barrier, waits)

    def thinned(ref, at, raw):
        return ref.at[at] if raw else ref.at[at, pl.ds(0, thin)]

    def to_right(at, raw):
        return pltpu.make_async_remote_copy(
            src_ref=cube.at[at] if raw else for_both.at[at, pl.ds(thin, thin)], dst_ref=thinned(left_in, at, raw),
            send_sem=send_sem.at[0, at], recv_sem=recv_sem.at[0, at],
            device_id={"chan": group + 1}, device_id_type=MESH)

    def to_left(at, raw):
        return pltpu.make_async_remote_copy(
            src_ref=cube.at[at] if raw else for_both.at[at, pl.ds(0, thin)], dst_ref=thinned(right_in, at, raw),
            send_sem=send_sem.at[1, at], recv_sem=recv_sem.at[1, at],
            device_id={"chan": group - 1}, device_id_type=MESH)

    def send(at, raw):
        @pl.when(has_right)
        def _():
            to_right(at, raw).start()

        @pl.when(has_left)
        def _():
            to_left(at, raw).start()

    def send_pair(step, raw):
        send(step, raw)
        send(chunks - 1 - step, raw)

    def ask(side):
        return pltpu.make_async_remote_copy(
            src_ref=needs.at[side], dst_ref=asked.at[1 - side], send_sem=need_send.at[side],
            recv_sem=need_recv.at[1 - side], device_id=sides[side][1], device_id_type=MESH)

    def pass_on(way, hop):
        return pltpu.make_async_remote_copy(
            src_ref=my_flag.at[0] if hop == 0 else ring.at[way, hop - 1], dst_ref=ring.at[way, hop],
            send_sem=ring_send.at[way, hop], recv_sem=ring_recv.at[way, hop], device_id=around[way],
            device_id_type=MESH)

    def turn_ring(hop):
        if not lean or outer == 1 or hop > max(hops):
            return

        @pl.when(middle)
        def _():
            for way in range(2):
                if 0 < hop <= hops[way]:
                    pass_on(way, hop - 1).wait_recv()
                if hop < hops[way]:
                    pass_on(way, hop).start()

    inward = jnp.where(spot == 1, group + 1, group - 1)
    outward = jnp.where(spot == 1, group - 1, group + 1)

    def tell(stage, device):
        return pltpu.make_async_remote_copy(
            src_ref=my_flag.at[1 + stage], dst_ref=flag_in.at[stage], send_sem=flag_send.at[stage],
            recv_sem=flag_recv.at[stage], device_id=device, device_id_type=MESH)

    tells = (tell(0, facing), tell(1, {"chan": inward}), tell(2, {"chan": outward})) if lean else ()

    if lean:
        for side in range(2):
            @pl.when(sides[side][0])
            def _():
                ask(side).start()

    send(0, True)
    if not lean:
        send(chunks - 1, True)
        send_pair(1, True)

    @pl.when(jnp.logical_not(has_left))
    def _():
        left_in[...] = jnp.zeros(left_in.shape, F32)

    @pl.when(jnp.logical_not(has_right))
    def _():
        right_in[...] = jnp.zeros(right_in.shape, F32)

    for copy in local[3:]:
        copy.wait()

    def apply(op, value, rows_out):
        high, low = split(value)
        both = dot(op, high)
        return both[:rows_out] + both[rows_out:] + dot(op[:rows_out], low)

    def reduce_for(at):
        for_both[at] = apply(send_op[...], own[at], 2 * thin)

    pick = ones_where(iota((128, size), 0) == iota((128, size), 1) % chans)
    same_row = iota((size, size), 0) // chans == iota((size, size), 1) // chans
    for slot, band in enumerate(bands):
        for half, part in enumerate(split(band)):
            wide = jnp.concatenate([dot(part, pick)] * BAND, axis=0)
            chan_op[pl.ds(half * size, size), pl.ds(slot * size, size)] = jnp.where(same_row, wide, 0.0).astype(BF16)
    if lean:
        pick = ones_where(iota((128, 128), 0) == iota((128, 128), 1) // BAND)
        same_row = iota((size, 128), 0) // chans == iota((size, 128), 1) % BAND
        for side, (_, receive) in enumerate(receives):
            for half, part in enumerate(receive):
                wide = jnp.concatenate([dot(part, pick)] * BAND, axis=0)
                receive_ops[side, pl.ds(half * size, size), :] = jnp.where(same_row, wide, 0.0).astype(BF16)

        for side in range(2):
            @pl.when(sides[side][0])
            def _():
                ask(1 - side).wait_recv()

        my_flag[0] = needs[0, :8] + asked[0, :8] + asked[1, :8]
        pick = ones_where(iota((128, 128), 0) == iota((128, 128), 1) % chans)
        same_row = iota((128, 128), 0) % BAND == iota((128, 128), 1) // chans
        for side in range(2):
            for half, part in enumerate(split(asked[side])):
                wide = jnp.broadcast_to(dot(part, pick)[:, None, :], (chans, BAND, 128)).reshape(128, 128)
                send_op[pl.ds((2 * half + side) * thin, thin), :] = jnp.where(same_row, wide, 0.0)[:thin].astype(BF16)
        reduce_for(chunks - 1)
        reduce_for(1)
        send(chunks - 1, False)
        turn_ring(0)
        reduce_for(chunks - 2)
        send(1, False)

    high, low = split(cols[...])
    cols_pair[0] = high
    cols_pair[1] = low
    turn_ring(1)

    pick = ones_where(iota((128, 3 * size), 0) == iota((128, 3 * size), 1) // chans)
    same_chan = iota((size, 3 * size), 0) % chans == iota((size, 3 * size), 1) % chans
    for at in range(chunks):
        start = height + (at - 1) * BAND
        close = rows[pl.ds(at * BAND, BAND), start:start + 3 * BAND]
        close = jnp.concatenate([close, jnp.zeros((BAND, 128 - 3 * BAND), F32)], axis=1)
        for half, part in enumerate(split(close)):
            wide = dot(part, pick)
            wide = jnp.broadcast_to(wide[:, None, :], (BAND, chans, 3 * size)).reshape(size, 3 * size)
            row_ops[at, pl.ds(half * size, size), :] = jnp.where(same_chan, wide, 0.0).astype(BF16)

    if lean:
        turn_ring(2)
        reduce_for(2)
        send(chunks - 2, False)

    def keep(at, value):
        high, low = split(value)
        spread[at] = high
        spread_low[at] = low

    def arrive(at, raw):
        @pl.when(has_left)
        def _():
            to_right(at, raw).wait_recv()

        @pl.when(has_right)
        def _():
            to_left(at, raw).wait_recv()

    def blend(part, ref, at, raw=True):
        if raw:
            return apply(chan_op[:, part * size:(part + 1) * size], ref[at], size)
        return apply(receive_ops[part // 2, :, :thin], ref[at, pl.ds(0, thin)], size)

    def across(total):
        high, low = split(total)
        both = dot_across(jnp.concatenate([high, low], axis=0), cols_pair[0])
        return both[:size] + both[size:] + dot_across(high, cols_pair[1])

    def smooth(at, raw):
        arrive(at, raw)
        return across(blend(1, own, at) + blend(0, left_in, at, raw) + blend(2, right_in, at, raw))

    def finish(at):
        op = row_ops[at]
        both = dot(op, spread[pl.ds(at, 3)].reshape(3 * size, width))
        out[at] = both[:size] + both[size:] + dot(op[:size], spread_low[pl.ds(at, 3)].reshape(3 * size, width))

    whole = not lean
    for side, at in enumerate((0, chunks - 1)):
        value = smooth(at, at == 0 or whole)
        edge_out[side] = value
        keep(at + 1, value)
        if lean:
            turn_ring(3 + side)
            reduce_for((chunks - 3, 3)[side])
            send((2, chunks - 3)[side], False)
    if lean:
        for hop in range(5, max(hops) + 1):
            turn_ring(hop)

        @pl.when(middle)
        def _():
            total = my_flag[0]
            for way in range(2):
                for hop in range(hops[way]):
                    total = total + ring[way, hop]
            my_flag[1] = total

    def edge(side, device):
        return pltpu.make_async_remote_copy(
            src_ref=edge_out.at[side], dst_ref=edge_in.at[1 - side], send_sem=edge_send.at[side],
            recv_sem=edge_recv.at[1 - side], device_id=device, device_id_type=MESH)

    up, down = edge(0, {"sky": sky - 1}), edge(1, {"sky": sky + 1})

    def first_leg(side):
        return pltpu.make_async_remote_copy(
            src_ref=edge_out.at[side], dst_ref=detour, send_sem=edge_send.at[side], recv_sem=edge_recv.at[2],
            device_id={"chan": beside}, device_id_type=MESH)

    def second_leg(side):
        return pltpu.make_async_remote_copy(
            src_ref=detour, dst_ref=edge_in.at[1 - side], send_sem=edge_send.at[2],
            recv_sem=edge_recv.at[1 - side], device_id={"chan": served, "sky": beyond}, device_id_type=MESH)

    turns = ((0, jnp.logical_not(odd)), (1, odd))
    for side, turn in turns:
        there, copy = ((has_up, up), (has_down, down))[side]

        @pl.when(there & jnp.logical_not(detours & turn))
        def _():
            copy.start()

        @pl.when(detours & turn)
        def _():
            first_leg(side).start()

    if lean:
        reduce_for(chunks - 4)
        send(3, False)
        if inner > RUN:
            @pl.when(middle)
            def _():
                tells[0].start()

        reduce_for(4)
        send(chunks - 4, False)
    else:
        for step in range(2, AHEAD + 2):
            send_pair(step, True)
    keep(2, smooth(1, whole))
    if lean:
        @pl.when(middle)
        def _():
            total = my_flag[1]
            if inner > RUN:
                tells[0].wait_recv()
                total = total + flag_in[0]
            my_flag[2] = total

    keep(chunks - 1, smooth(chunks - 2, whole))
    if lean:
        @pl.when(middle)
        def _():
            tells[1].start()

        @pl.loop(4, last)
        def _(step):
            reduce_for(chunks - 1 - step)
            send(step, False)

            @pl.when(step < last - 1)
            def _():
                reduce_for(step + 1)
                send(chunks - 1 - step, False)

    keep(last + 1, jnp.zeros((size, width), F32))
    for spot in range(3):
        for half in range(2):
            tail_op[pl.ds((3 * half + spot) * size, size), :] = row_ops[
                last - 1 + spot, pl.ds(half * size, size), (2 - spot) * size:(3 - spot) * size]

    def tend(step):
        if not lean:
            @pl.when(step + AHEAD < last)
            def _():
                send_pair(step + AHEAD, True)

        for at in (step, chunks - 1 - step):
            keep(at + 1, smooth(at, whole))
        finish(step - 1)
        finish(chunks - step)

    tend(2)
    if lean:
        send(last, False)

    @pl.loop(3, last - 3)
    def _(step):
        tend(step)

    if lean:
        @pl.when(middle)
        def _():
            tells[1].wait_recv()
            my_flag[3] = my_flag[2] + flag_in[1]

    for side, turn in turns:
        @pl.when(relays & turn)
        def _():
            first_leg(side).wait_recv()
            second_leg(side).start()

    @pl.loop(last - 3, last - 1)
    def _(step):
        tend(step)

    @pl.when(has_up)
    def _():
        down.wait_recv()
        keep(0, edge_in[0])

    @pl.when(has_down)
    def _():
        up.wait_recv()
        keep(chunks + 1, edge_in[1])

    @pl.when(jnp.logical_not(has_up))
    def _():
        keep(0, jnp.zeros((size, width), F32))

    @pl.when(jnp.logical_not(has_down))
    def _():
        keep(chunks + 1, jnp.zeros((size, width), F32))

    finish(0)
    finish(chunks - 1)
    finish(last + 1)
    keep(last, smooth(last - 1, whole))
    if lean:
        @pl.when(middle)
        def _():
            tells[2].start()
            flag[...] = my_flag[3, :1, 64:65]

    ready = blend(1, own, last)
    for at in (last - 2, last - 1, last):
        finish(at)

    arrive(last, whole)
    high, low = split(across(ready + blend(0, left_in, last, whole) + blend(2, right_in, last, whole)))
    three = 3 * size
    both = dot(tail_op[...], high)
    share = both[:three] + both[three:] + dot(tail_op[:three, :], low)
    for spot in range(3):
        out[last - 1 + spot] += share[spot * size:(spot + 1) * size]

    if lean:
        @pl.when(jnp.logical_not(middle))
        def _():
            tells[2].wait_recv()
            flag[...] = flag_in[2, :1, 64:65]

        @pl.when(middle)
        def _():
            for copy in tells[inner == RUN:]:
                copy.wait_send()
            if outer > 1:
                for way in range(2):
                    for hop in range(hops[way]):
                        pass_on(way, hop).wait_send()

    for side, turn in turns:
        @pl.when(relays & turn)
        def _():
            second_leg(side).wait_send()

    for (there, _), wait in zip(sides[2:], (up, down)):
        @pl.when(there)
        def _():
            wait.wait_send()

    if lean:
        for side in range(2):
            @pl.when(sides[side][0])
            def _():
                ask(side).wait_send()

    def sent(at, raw):
        @pl.when(has_right)
        def _():
            to_right(at, raw).wait_send()

        @pl.when(has_left)
        def _():
            to_left(at, raw).wait_send()

    sent(0, True)

    @pl.loop(1, chunks)
    def _(at):
        sent(at, whole)


def store(x):
    pieces = 4

    def body(x_ref, out_ref, sem):
        step = x.shape[0] // pieces
        copies = [pltpu.make_async_copy(x_ref.at[pl.ds(at * step, step)], out_ref.at[pl.ds(at * step, step)], sem.at[at])
                  for at in range(pieces)]
        for copy in copies:
            copy.start()
        for copy in copies:
            copy.wait()

    return pl.pallas_call(
        body, out_shape=pltpu.HBM(x.shape, x.dtype), in_specs=[pl.BlockSpec(memory_space=pltpu.VMEM)],
        out_specs=pl.BlockSpec(memory_space=pltpu.HBM), scratch_shapes=[pltpu.SemaphoreType.DMA((pieces,))],
        compiler_params=pltpu.CompilerParams(vmem_limit_bytes=1 << 20), name="store",
    )(pltpu.with_memory_space_constraint(x, pltpu.VMEM))


def solution(mesh):
    groups, skies = mesh.shape["chan"], mesh.shape["sky"]

    def regrid(lean, cube, shifts, halfwidth, taps, beam_rows, beam_cols):
        chunks, size, width = cube.shape
        height, chans = chunks * BAND, size // BAND
        thin = SLOTS * BAND
        inner = min(INNER, groups)
        outer = groups // inner
        whole = (chunks, size, width)
        vmem = pl.BlockSpec(memory_space=pltpu.VMEM)
        results, extra = [pltpu.VMEM(whole, F32)], []
        if lean:
            results.append(jax.ShapeDtypeStruct((1, 1), F32))
            extra = [
                pltpu.VMEM((2, chans, 128), F32),
                pltpu.VMEM((2, chans, 128), F32),
                pltpu.VMEM((chunks, 2 * thin, width), F32),
                pltpu.VMEM((4 * thin, 128), BF16),
                pltpu.VMEM((2, 2 * size, 128), BF16),
                pltpu.VMEM((4, 8, 128), F32),
                pltpu.VMEM((2, max(outer // 2, 1), 8, 128), F32),
                pltpu.VMEM((3, 8, 128), F32),
                pltpu.SemaphoreType.DMA((2,)),
                pltpu.SemaphoreType.DMA((2,)),
                pltpu.SemaphoreType.DMA((2, max(outer // 2, 1))),
                pltpu.SemaphoreType.DMA((2, max(outer // 2, 1))),
                pltpu.SemaphoreType.DMA((3,)),
                pltpu.SemaphoreType.DMA((3,)),
            ]
        return pl.pallas_call(
            functools.partial(kernel, lean, groups, skies),
            out_shape=results,
            in_specs=[pl.BlockSpec(memory_space=pltpu.HBM)] * 6,
            out_specs=[vmem] * len(results),
            scratch_shapes=extra + [
                pltpu.SMEM(shifts.shape, jnp.int32),
                pltpu.SMEM(halfwidth.shape, jnp.int32),
                pltpu.VMEM(taps.shape, F32),
                pltpu.VMEM(whole, F32),
                pltpu.VMEM(whole, F32),
                pltpu.VMEM(whole, F32),
                pltpu.VMEM((chunks + 2, size, width), BF16),
                pltpu.VMEM((chunks + 2, size, width), BF16),
                pltpu.VMEM((6 * size, size), BF16),
                pltpu.VMEM((2, size, width), F32),
                pltpu.VMEM((2, size, width), F32),
                pltpu.VMEM((size, width), F32),
                pltpu.VMEM((width, width), F32),
                pltpu.VMEM((2, width, width), BF16),
                pltpu.VMEM((height, 3 * height), F32),
                pltpu.VMEM((chunks, 2 * size, 3 * size), BF16),
                pltpu.VMEM((2 * size, 3 * size), BF16),
                pltpu.SemaphoreType.DMA((8,)),
                pltpu.SemaphoreType.DMA((2, chunks)),
                pltpu.SemaphoreType.DMA((2, chunks)),
                pltpu.SemaphoreType.DMA((3,)),
                pltpu.SemaphoreType.DMA((3,)),
            ],
            compiler_params=pltpu.CompilerParams(
                collective_id=int(lean), has_side_effects=True, vmem_limit_bytes=40 << 20),
            name="regrid" if lean else "regrid_whole",
        )(*(pltpu.with_memory_space_constraint(x, pltpu.HBM) for x in (
            cube, shifts, halfwidth, taps, beam_rows, beam_cols)))

    def per_device(cube, *others):
        height, chans, width = cube.shape
        args = (cube.reshape(height // BAND, BAND * chans, width), *others)
        result, flag = regrid(True, *args)
        result, _ = lax.while_loop(
            lambda state: state[1] > 0.5,
            lambda state: (store(regrid(False, *args)[0]), jnp.zeros((), F32)),
            (store(result), flag[0, 0]))
        return result.reshape(cube.shape)

    return jax.shard_map(
        per_device,
        mesh=mesh,
        in_specs=(P("sky", "chan", None), P("chan"), P("chan"), P("chan", None), P(), P()),
        out_specs=P("sky", "chan", None),
        check_vma=False,
    )
```
